128 devices in a mesh: hyp: 2 (over core), tm: 64 (over y, z, x).
Axes of the slice: x: 4, y: 4, z: 4, core: 2. Of those that a mesh axis runs over, the one named last changes fastest.
Arguments:
- damping: float32 [256, 384], P(('hyp', 'tm')), parts along dimension 0, may hold values from 0.0002 to 0.002
- spatial_factor: float32 [256, 384, 384], P(('hyp', 'tm')), parts along dimension 0, may hold values from -0.3125 to 0.3125
- edge_scale: float32 [256, 384], P(('hyp', 'tm')), parts along dimension 0, may hold values from 1 to 4
- edge_factor: float32 [256, 384, 384], P(('hyp', 'tm')), parts along dimension 0, may hold values from -0.3125 to 0.3125
- forcing: float32 [256, 384], P(('hyp', 'tm')), parts along dimension 0, may hold values from -6 to 6
Outputs:
- solution: float32 [256, 384], P(('hyp', 'tm')), parts along dimension 0
- logdet_mean: float32 [2], P('hyp'), parts along dimension 0
The draws below stay inside these ranges and needn't reach their ends.
There are 2 independent parts, one for each index of `hyp`. The reference program is written for one: setup_inputs(seed, part) draws one part's arguments, and reference() takes and returns one part's arrays. A program takes and returns all parts, laid end to end along the dimension named above; each array names one. Nothing has to cross between parts.
All inputs are finite; a program needn't handle non-finite values.
Results may differ from the reference program's by a relative error of at most 0.0003.
Values sent between devices are 32-bit elements; how exact they have to be, the bound alone decides.
No kernel may reach another device: no remote copies, remote signals or barrier semaphores. Data moves between devices by JAX's collectives and lax.ppermute only.
A program may use at most 256 MiB of HBM per device.

```python
import math
import jax
import jax.numpy as jnp
from jax import lax

NODES = 384
STEPS = 128


def block_levels(key, extent, shards, smallest, top_value):
    gain = 1.0
    for dim, parts in shards:
        steps = jax.random.uniform(jax.random.fold_in(jax.random.fold_in(key, 6), dim), (parts,), jnp.float32, smallest / len(shards), top_value / len(shards))
        gain = gain * jnp.repeat(jnp.exp(steps), extent[dim] // parts).reshape((-1,) + (1,) * (len(extent) - 1 - dim))
    return gain


def scatter_about(own_key, dims, width, most, shards=(), held_as=jnp.bfloat16):
    result = jax.random.normal(own_key, dims, jnp.float32) * width
    if len(shards) > 0:
        result = block_levels(own_key, dims, shards, -0.22, 0.18) * result
    return jnp.clip(result, min=-most, max=most).astype(held_as)


def setup_inputs(seed: int = 0, part: int = 0) -> dict:
    arg_keys = jax.random.split(jax.random.key(seed), 6)
    part_keys = jax.random.split(jax.random.fold_in(arg_keys[5], part), 6)
    return {
        "damping": jnp.clip(jnp.exp(math.log(0.002) - 2.3025852 * jax.random.uniform(part_keys[0], (STEPS, NODES), jnp.float32) ** block_levels(part_keys[0], (STEPS, NODES), ((0, 64),), -0.2, 0.2)), 0.0002, 0.002),
        "spatial_factor": scatter_about(part_keys[1], (STEPS, NODES, NODES), NODES ** -0.5, 0.3125, ((0, 64),), jnp.float32),
        "edge_scale": jnp.clip(jnp.exp(math.log(4.0) - 1.3862944 * jax.random.uniform(part_keys[2], (STEPS, NODES), jnp.float32) ** block_levels(part_keys[2], (STEPS, NODES), ((0, 64),), -0.2, 0.2)), 1.0, 4.0),
        "edge_factor": scatter_about(part_keys[3], (STEPS, NODES, NODES), NODES ** -0.5, 0.3125, ((0, 64),), jnp.float32),
        "forcing": scatter_about(part_keys[4], (STEPS, NODES), 1.0, 6.0, ((0, 64),), jnp.float32),
    }


spatial_gain = 0.02

def matmul(former, latter):
    return jnp.dot(former, latter, precision=lax.Precision.HIGHEST)

def reference(damping, spatial_factor, edge_scale, edge_factor, forcing):
    time_blocks, width_nodes = forcing.shape
    edge_mats = jax.vmap(jnp.diag)(edge_scale) + jnp.einsum('tij,tkj->tik', edge_factor, edge_factor, precision=lax.Precision.HIGHEST)
    spatial = jnp.einsum('tij,tkj->tik', spatial_factor, spatial_factor, precision=lax.Precision.HIGHEST)
    shifted = jnp.concatenate([jnp.zeros_like(edge_mats[:1]), edge_mats[:-1]], axis=0)
    squares = jax.vmap(jnp.diag)(damping) + spatial_gain * spatial + edge_mats + shifted

    def forward(carry, inputs):
        below, carried = carry
        square, onward, source = inputs
        schur = square - matmul(below, below.T)
        factor = jnp.linalg.cholesky(schur)
        solved = jax.scipy.linalg.solve_triangular(factor, source - matmul(below, carried), lower=True)
        next_below = jax.scipy.linalg.solve_triangular(factor, -onward, lower=True).T
        return ((next_below, solved), (factor, next_below, solved))
    start = (jnp.zeros((width_nodes, width_nodes), jnp.float32), jnp.zeros((width_nodes,), jnp.float32))
    _, (factors, belows, solveds) = lax.scan(forward, start, (squares, edge_mats, forcing))

    def backward(later, inputs):
        factor, below, solved = inputs
        value = jax.scipy.linalg.solve_triangular(factor, solved - matmul(below.T, later), lower=True, trans=1)
        return (value, value)
    _, solution = lax.scan(backward, jnp.zeros((width_nodes,), jnp.float32), (factors, belows, solveds), reverse=True)
    logdet = 2.0 * jnp.sum(jnp.log(jnp.diagonal(factors, axis1=1, axis2=2)))
    return (solution, jnp.reshape(logdet / (time_blocks * width_nodes), (1,)))
```

```python
import jax
import jax.numpy as jnp
from jax import lax
from jax.experimental import pallas as pl
from jax.experimental.pallas import tpu as pltpu
from jax.sharding import PartitionSpec as P

N = 384
B = 128
spatial_gain = 0.02
f32 = jnp.float32
bf16 = jnp.bfloat16
NN = (((1,), (0,)), ((), ()))
NT = (((1,), (1,)), ((), ()))
BLOCKS = ((0, 0), (1, 0), (1, 1), (2, 0), (2, 1), (2, 2))
ROWS = 6 * B + 24
TALL = 2 * N
LOG_COEFS = (0.999973924, -0.499286916, 0.326642792, -0.219344301, 0.120321356, -0.037876697, 0.002717324)


def split3(x):
    top, rest = split2_wide(x)
    middle, last = split2_wide(rest)
    return top, middle, last.astype(bf16)


def split2_wide(x):
    top = x.astype(bf16)
    return top, x - top.astype(f32)


def dot_hi(a, b, dims=NN):
    a1, a2, a3 = split3(a)
    b1, b2, b3 = split3(b)
    return lax.dot_general(
        jnp.concatenate([a1, a1, a2, a2, a1, a3], axis=1),
        jnp.concatenate([b1, b2, b1, b2, b3, b1], axis=dims[0][1][0]),
        dims,
        preferred_element_type=f32,
    )


def dot_one(a, b):
    return jnp.dot(a.astype(bf16), b.astype(bf16), preferred_element_type=f32)


def split2(x):
    top = x.astype(bf16)
    return top, (x - top.astype(f32)).astype(bf16)


def dot_three(a, b):
    a1, a2 = split2(a)
    b1, b2 = split2(b)
    return jnp.dot(
        jnp.concatenate([a1, a1, a2], axis=1),
        jnp.concatenate([b1, b2, b1], axis=0),
        preferred_element_type=f32,
    )


def eye_mask():
    return lax.broadcasted_iota(jnp.int32, (N, N), 0) == lax.broadcasted_iota(jnp.int32, (N, N), 1)


def total(x):
    return jnp.sum(x)


def unpack(ref):
    blocks = {}
    for k, (i, j) in enumerate(BLOCKS):
        block = ref[k * B : (k + 1) * B, :]
        blocks[i, j] = block
        if i != j:
            blocks[j, i] = block.T
    return jnp.concatenate(
        [jnp.concatenate([blocks[i, j] for j in range(3)], axis=1) for i in range(3)], axis=0
    )


def unpack_vector(ref):
    return jnp.concatenate([ref[6 * B + 8 * k : 6 * B + 8 * k + 8, :] for k in range(3)], axis=1)


def pack(ref, square, vector):
    for k, (i, j) in enumerate(BLOCKS):
        ref[k * B : (k + 1) * B, :] = square[i * B : (i + 1) * B, j * B : (j + 1) * B]
    for k in range(3):
        ref[6 * B + 8 * k : 6 * B + 8 * k + 8, :] = vector[:, k * B : (k + 1) * B]


def newton_inverse(a):
    eye = eye_mask()
    diag_col = jnp.sum(jnp.where(eye, a, 0.0), axis=1, keepdims=True)
    diag_row = jnp.sum(jnp.where(eye, a, 0.0), axis=0, keepdims=True)
    inv_col = 1.0 / diag_col
    inv_row = 1.0 / diag_row
    high = jnp.max(jnp.sum(jnp.abs(a), axis=1, keepdims=True) * inv_col)
    ratio = 10.0
    width = 1.0 - 1.0 / ratio
    centre = (1.0 + 1.0 / ratio) / width
    bound = 1.0 / (2.0 * centre * centre - 1.0)
    alpha = 8.0 * centre * bound / (width * high)
    beta = -8.0 * bound / (width * width * high * high)
    x = beta * (inv_col * a * inv_row) + jnp.where(eye, alpha * inv_row, 0.0)
    one = jnp.where(eye, 1.0, 0.0)
    a_low = a.astype(bf16)
    for _ in range(2):
        half = 0.5 * bound * bound
        gain = 1.0 / (1.0 - half)
        bound = half * gain
        r = one - jnp.dot(a_low, x.astype(bf16), preferred_element_type=f32)
        x = gain * (x + dot_one(x, r))
    r = one - dot_three(a, x)
    x = x + dot_one(x, r)

    def more(carry):
        return jnp.logical_and(carry[1] > 1e-5, carry[0] < 40)

    def step(carry):
        count, _, x = carry
        r = jnp.where(eye_mask(), 1.0, 0.0) - dot_hi(a, x)
        return count + 1, total(r * r), x + dot_three(x, r)

    return lax.while_loop(more, step, (jnp.int32(0), jnp.float32(1.0), x))[2]


def log_det(a):
    eye = eye_mask()
    diag_col = jnp.sum(jnp.where(eye, a, 0.0), axis=1, keepdims=True)
    diag_row = jnp.sum(jnp.where(eye, a, 0.0), axis=0, keepdims=True)
    scaled = lax.rsqrt(diag_col) * a * lax.rsqrt(diag_row)
    high = jnp.max(jnp.sum(jnp.abs(scaled), axis=1, keepdims=True))
    base = total(jnp.log(diag_row)) + N * jnp.max(jnp.log(jnp.full((8, B), high)))
    r = jnp.where(eye, 1.0, 0.0) - scaled * (1.0 / high)
    r2 = dot_hi(r, r)

    def more(carry):
        return jnp.logical_and(carry[1] > 1e-4, carry[0] < 40)

    def step(carry):
        count, trace, value, r, r2 = carry
        r4 = dot_hi(r2, r2)
        c1, c2, c3, c4, c5, c6, c8 = LOG_COEFS
        terms = r * (c2 * r + c3 * r2 + c5 * r4) + r2 * (c4 * r2 + c6 * r4) + c8 * (r4 * r4)
        value = value + c1 * trace + total(terms)
        return count + 1, total(jnp.where(eye_mask(), r2, 0.0)), value, r2, r4

    trace = total(jnp.where(eye, r, 0.0))
    _, trace, value, _, _ = lax.while_loop(more, step, (jnp.int32(0), trace, jnp.float32(0.0), r, r2))
    return base - value - trace


def diagonal(row):
    return jnp.where(eye_mask(), row, 0.0)


def first_kernel(flag, damping, spatial, scales, factors, source, message, root, edges, fold, local, packed):
    before = diagonal(scales[0:1, :]) + dot_hi(factors[0], factors[0], NT)
    after = diagonal(scales[1:2, :]) + dot_hi(factors[1], factors[1], NT)
    square = diagonal(damping[1:2, :]) + spatial_gain * dot_hi(spatial[0], spatial[0], NT) + after + before
    edges[0:N, :] = before
    after_out = jnp.where(flag[0] > 0, after, 0.0)
    edges[N:TALL, :] = after_out
    inverse = newton_inverse(square)
    vector = jnp.broadcast_to(source[1:2, :], (8, N))
    pack(packed, square, vector)
    root[...] = inverse
    z = dot_hi(vector, inverse)
    local[...] = z
    right = dot_hi(after_out, inverse)
    fold[...] = right
    pack(message, after_out - dot_hi(right, after_out, NT), dot_hi(z, after_out, NT))


def first_link_kernel(flag, root, edges, right, stack, link):
    left = dot_hi(edges[0:N, :], root[...])
    stack[0:N, :] = left
    stack[N:TALL, :] = right[...]

    @pl.when(flag[0] > 0)
    def _():
        link[...] = dot_hi(right[...], edges[0:N, :], NT)

    @pl.when(flag[0] == 0)
    def _():
        link[...] = dot_hi(left, edges[N:TALL, :], NT)


def first_own_kernel(damping, spatial, source, edges, stack, local, state):
    before = edges[0:N, :]
    square = diagonal(damping[0:1, :]) + spatial_gain * dot_hi(spatial[0], spatial[0], NT) + before
    vector = jnp.broadcast_to(source[0:1, :], (8, N)) + dot_hi(local[...], before, NT)
    pack(state, square - dot_hi(stack[0:N, :], before, NT), vector)


def invert_kernel(flag, state, left, right, prior, new_state, inverse, local):
    new_state[...] = state[...] + left[...] + right[...]
    local[...] = prior[...]

    @pl.when(flag[0] > 0)
    def _():
        inv = newton_inverse(unpack(new_state))
        inverse[...] = inv
        local[...] = dot_hi(unpack_vector(new_state), inv)


def product_kernel(flag, inverse, local, near, far, prior, stack, left, right):
    @pl.when(flag[0] > 0)
    def _():
        z = local[...]
        part = dot_hi(near[...], inverse[...])
        stack[0:N, :] = part
        pack(left, -dot_hi(part, near[...], NT), dot_hi(z, near[...], NT))
        part = dot_hi(far[...], inverse[...])
        stack[N:TALL, :] = part
        pack(right, -dot_hi(part, far[...], NT), dot_hi(z, far[...], NT))


def link_kernel(flag, side, stack, near, far, link):
    @pl.when(jnp.logical_and(flag[0] > 0, side[0] > 0))
    def _():
        link[...] = dot_hi(stack[N:TALL, :], near[...], NT)

    @pl.when(jnp.logical_and(flag[0] > 0, side[0] == 0))
    def _():
        link[...] = dot_hi(stack[0:N, :], far[...], NT)


def log_kernel(flag, packed, prior, logs):
    logs[...] = prior[...]

    @pl.when(flag[0] > 0)
    def _():
        logs[...] = prior[...] + log_det(unpack(packed))


def descend_kernel(flag, local, stack, left, right, current, value):
    value[...] = current[...]

    @pl.when(flag[0] > 0)
    def _():
        both = jnp.concatenate([left[...], right[...]], axis=1)
        value[...] = local[...] + dot_hi(both, stack[...])


SMEM = pl.BlockSpec(memory_space=pltpu.SMEM)
VMEM = pl.BlockSpec(memory_space=pltpu.VMEM)


def shape(*dims):
    return jax.ShapeDtypeStruct(dims, f32)


def call(kernel, name, outs, specs, args, aliases={}):
    return pl.pallas_call(
        kernel,
        name=name,
        out_shape=outs,
        in_specs=specs,
        out_specs=[VMEM] * len(outs),
        input_output_aliases=aliases,
        compiler_params=pltpu.CompilerParams(vmem_limit_bytes=48 << 20),
    )(*args)


def local(damping, spatial_factor, edge_scale, edge_factor, forcing):
    size = lax.axis_size("tm")
    position = lax.axis_index("tm")

    def flag(condition):
        return jnp.reshape(condition.astype(jnp.int32), (1,))

    def send(x, pairs):
        return lax.ppermute(x, "tm", [p for p in pairs if 0 <= p[1] < size])

    message, root, edges, right, local1, packed = call(
        first_kernel,
        "first",
        [shape(ROWS, B), shape(N, N), shape(TALL, N), shape(N, N), shape(8, N), shape(ROWS, B)],
        [SMEM] + [VMEM] * 5,
        (flag(position < size - 1), damping, spatial_factor[1:2], edge_scale, edge_factor, forcing),
    )
    from_left = send(message, [(i, i + 1) for i in range(size)])
    stack1, link = call(
        first_link_kernel,
        "first_link",
        [shape(TALL, N), shape(N, N)],
        [SMEM] + [VMEM] * 3,
        (flag(position % 2 == 1), root, edges, right),
    )
    near = send(link, [(i, i + 1) for i in range(0, size, 2)])
    far = link
    (state,) = call(
        first_own_kernel,
        "first_own",
        [shape(ROWS, B)],
        [VMEM] * 6,
        (damping, spatial_factor[0:1], forcing, edges, stack1, local1),
    )
    logs = jnp.zeros((8, B), f32)
    stack = jnp.zeros((TALL, N), f32)
    own = jnp.zeros((8, N), f32)
    from_right = jnp.zeros((ROWS, B), f32)
    always = jnp.ones((1,), jnp.int32)
    span = 1
    while span < size:
        step = 2 * span
        active = flag(position % step == span)
        side = flag((position // step) % 2 == 1)
        state, inverse, own = call(
            invert_kernel,
            "invert",
            [shape(ROWS, B), shape(N, N), shape(8, N)],
            [SMEM] + [VMEM] * 4,
            (active, state, from_left, from_right, own),
            {4: 2},
        )
        stack, to_left, to_right = call(
            product_kernel,
            "product",
            [shape(TALL, N), shape(ROWS, B), shape(ROWS, B)],
            [SMEM] + [VMEM] * 5,
            (active, inverse, own, near, far, stack),
            {5: 0},
        )
        odd = range(span, size, step)
        from_right = send(to_left, [(i, i - span) for i in odd])
        if step < size:
            from_left = send(to_right, [(i, i + span) for i in odd])
            (link,) = call(
                link_kernel,
                "link",
                [shape(N, N)],
                [SMEM] * 2 + [VMEM] * 3,
                (active, side, stack, near, far),
            )
            near = send(link, [(i, i + span) for i in odd if (i // step) % 2 == 0])
            far = send(link, [(i, i - span) for i in odd if (i // step) % 2 == 1])
        else:
            from_left = jnp.zeros((ROWS, B), f32)
        if span == 1:
            (logs,) = call(log_kernel, "log", [shape(8, B)], [SMEM, VMEM, VMEM], (always, packed, logs), {2: 0})
        if span == 8:
            (logs,) = call(
                log_kernel, "log", [shape(8, B)], [SMEM, VMEM, VMEM], (flag(position % 8 != 0), state, logs), {2: 0}
            )
        if step == size:
            (logs,) = call(
                log_kernel,
                "log",
                [shape(8, B)],
                [SMEM, VMEM, VMEM],
                (flag(jnp.logical_and(position % 8 == 0, position > 0)), state, logs),
                {2: 0},
            )
        span = step
    at_root = flag(position == 0)
    state, inverse, own = call(
        invert_kernel,
        "invert",
        [shape(ROWS, B), shape(N, N), shape(8, N)],
        [SMEM] + [VMEM] * 4,
        (at_root, state, from_left, from_right, own),
        {4: 2},
    )
    (logs,) = call(log_kernel, "log", [shape(8, B)], [SMEM, VMEM, VMEM], (at_root, state, logs), {2: 0})
    value = jnp.where(position == 0, own, 0.0)
    log_row = logs[0:1]
    while span > 1:
        step = span
        span //= 2
        odd = range(span, size, step)
        active = flag(position % step == span)
        left_value = send(value, [(i - span, i) for i in odd])
        right_value = send(value, [(i + span, i) for i in odd if i + span < size])
        log_row = log_row + send(log_row, [(i, i ^ span) for i in range(size)])
        (value,) = call(
            descend_kernel,
            "descend",
            [shape(8, N)],
            [SMEM] + [VMEM] * 5,
            (active, own, stack, left_value, right_value, value),
            {5: 0},
        )
    right_value = send(value, [(i + 1, i) for i in range(size - 1)])
    (second,) = call(
        descend_kernel,
        "descend",
        [shape(8, N)],
        [SMEM] + [VMEM] * 5,
        (always, local1, stack1, value, right_value, jnp.zeros((8, N), f32)),
        {5: 0},
    )
    solution = jnp.concatenate([value[0:1], second[0:1]], axis=0)
    logdet_mean = log_row[0, 0:1] / (size * 2 * N)
    return (solution, logdet_mean)


def solution(mesh):
    return jax.shard_map(
        local,
        mesh=mesh,
        in_specs=(
            P(("hyp", "tm"), None),
            P(("hyp", "tm"), None, None),
            P(("hyp", "tm"), None),
            P(("hyp", "tm"), None, None),
            P(("hyp", "tm"), None),
        ),
        out_specs=(P(("hyp", "tm"), None), P("hyp")),
        check_vma=False,
    )
```

```python
import jax
import jax.numpy as jnp
from jax import lax
from jax.experimental import pallas as pl
from jax.experimental.pallas import tpu as pltpu
from jax.sharding import PartitionSpec as P

N = 384
B = 128
spatial_gain = 0.02
f32 = jnp.float32
bf16 = jnp.bfloat16
NN = (((1,), (0,)), ((), ()))
NT = (((1,), (1,)), ((), ()))
BLOCKS = ((0, 0), (1, 0), (1, 1), (2, 0), (2, 1), (2, 2))
ROWS = 6 * B + 24
TALL = 2 * N
VMEM_LIMIT = 60 << 20
LOG_COEFS = (0.999973924, -0.499286916, 0.326642792, -0.219344301, 0.120321356, -0.037876697, 0.002717324)


def split3(x):
    top, rest = split2_wide(x)
    middle, last = split2_wide(rest)
    return top, middle, last.astype(bf16)


def split2_wide(x):
    top = x.astype(bf16)
    return top, x - top.astype(f32)


def dot_hi(a, b, dims=NN):
    a1, a2, a3 = split3(a)
    b1, b2, b3 = split3(b)
    return lax.dot_general(
        jnp.concatenate([a1, a1, a2, a2, a1, a3], axis=1),
        jnp.concatenate([b1, b2, b1, b2, b3, b1], axis=dims[0][1][0]),
        dims,
        preferred_element_type=f32,
    )


def dot_one(a, b):
    return jnp.dot(a.astype(bf16), b.astype(bf16), preferred_element_type=f32)


def split2(x):
    top = x.astype(bf16)
    return top, (x - top.astype(f32)).astype(bf16)


def dot_three(a, b):
    a1, a2 = split2(a)
    b1, b2 = split2(b)
    return jnp.dot(
        jnp.concatenate([a1, a1, a2], axis=1),
        jnp.concatenate([b1, b2, b1], axis=0),
        preferred_element_type=f32,
    )


def eye_mask(n=N):
    return lax.broadcasted_iota(jnp.int32, (n, n), 0) == lax.broadcasted_iota(jnp.int32, (n, n), 1)


def total(x):
    return jnp.sum(x)


def unpack(ref):
    blocks = {}
    for k, (i, j) in enumerate(BLOCKS):
        block = ref[k * B : (k + 1) * B, :]
        blocks[i, j] = block
        if i != j:
            blocks[j, i] = block.T
    return jnp.concatenate(
        [jnp.concatenate([blocks[i, j] for j in range(3)], axis=1) for i in range(3)], axis=0
    )


def unpack_vector(ref):
    return jnp.concatenate([ref[6 * B + 8 * k : 6 * B + 8 * k + 8, :] for k in range(3)], axis=1)


def pack(ref, square, vector):
    for k, (i, j) in enumerate(BLOCKS):
        ref[k * B : (k + 1) * B, :] = square[i * B : (i + 1) * B, j * B : (j + 1) * B]
    for k in range(3):
        ref[6 * B + 8 * k : 6 * B + 8 * k + 8, :] = vector[:, k * B : (k + 1) * B]


def newton_inverse(a):
    eye = eye_mask()
    diag_col = jnp.sum(jnp.where(eye, a, 0.0), axis=1, keepdims=True)
    diag_row = jnp.sum(jnp.where(eye, a, 0.0), axis=0, keepdims=True)
    inv_col = 1.0 / diag_col
    inv_row = 1.0 / diag_row
    high = jnp.max(jnp.sum(jnp.abs(a), axis=1, keepdims=True) * inv_col)
    ratio = 10.0
    width = 1.0 - 1.0 / ratio
    centre = (1.0 + 1.0 / ratio) / width
    bound = 1.0 / (2.0 * centre * centre - 1.0)
    alpha = 8.0 * centre * bound / (width * high)
    beta = -8.0 * bound / (width * width * high * high)
    x = beta * (inv_col * a * inv_row) + jnp.where(eye, alpha * inv_row, 0.0)
    one = jnp.where(eye, 1.0, 0.0)
    a_low = a.astype(bf16)
    for _ in range(2):
        half = 0.5 * bound * bound
        gain = 1.0 / (1.0 - half)
        bound = half * gain
        r = one - jnp.dot(a_low, x.astype(bf16), preferred_element_type=f32)
        x = gain * (x + dot_one(x, r))
    r = one - dot_three(a, x)
    x = x + dot_one(x, r)

    def more(carry):
        return jnp.logical_and(carry[1] > 1e-5, carry[0] < 40)

    def step(carry):
        count, _, x = carry
        r = jnp.where(eye_mask(), 1.0, 0.0) - dot_hi(a, x)
        return count + 1, total(r * r), x + dot_three(x, r)

    return lax.while_loop(more, step, (jnp.int32(0), jnp.float32(1.0), x))[2]


def log_start(a):
    n = a.shape[0]
    eye = eye_mask(n)
    diag_col = jnp.sum(jnp.where(eye, a, 0.0), axis=1, keepdims=True)
    diag_row = jnp.sum(jnp.where(eye, a, 0.0), axis=0, keepdims=True)
    scaled = lax.rsqrt(diag_col) * a * lax.rsqrt(diag_row)
    high = jnp.max(jnp.sum(jnp.abs(scaled), axis=1, keepdims=True))
    base = total(jnp.log(diag_row)) + n * jnp.max(jnp.log(jnp.full((8, B), high)))
    return base, jnp.where(eye, 1.0, 0.0) - scaled * (1.0 / high)


def log_terms(r, r2, r4):
    c1, c2, c3, c4, c5, c6, c8 = LOG_COEFS
    terms = r * (c2 * r + c3 * r2 + c5 * r4) + r2 * (c4 * r2 + c6 * r4) + c8 * (r4 * r4)
    return total(terms + c1 * jnp.where(eye_mask(r.shape[0]), r, 0.0))


def trace(r):
    return total(jnp.where(eye_mask(r.shape[0]), r, 0.0))


def log_det_ratio(a, b):
    base_a, ra = log_start(a)
    base_b, rb = log_start(b)

    def more(carry):
        return jnp.logical_and(carry[1] > 1e-4, carry[0] < 40)

    def step(carry):
        count, _, value, ra, ra2, rb, rb2 = carry
        ra4 = dot_hi(ra2, ra2)
        rb4 = dot_hi(rb2, rb2)
        value = value + log_terms(ra, ra2, ra4) - log_terms(rb, rb2, rb4)
        return count + 1, jnp.maximum(trace(ra2), trace(rb2)), value, ra2, ra4, rb2, rb4

    carry = (jnp.int32(0), jnp.float32(1.0), jnp.float32(0.0), ra, dot_hi(ra, ra), rb, dot_hi(rb, rb))
    _, _, value, ra, _, rb, _ = lax.while_loop(more, step, carry)
    return base_a - base_b - value - trace(ra) + trace(rb)


def diagonal(row):
    return jnp.where(eye_mask(), row, 0.0)


def copy_in(src, dst, sem):
    copy = pltpu.make_async_copy(src, dst, sem)
    copy.start()
    return copy


def first_kernel(
    flag, damping, scales, source, spatial, factors,
    message, root, edges, stack, local, packed,
    s_buf, f_buf, e_buf, w_buf, r_buf, m_buf, p_buf, sems,
):
    loads = [
        copy_in(factors.at[1], f_buf.at[1], sems.at[0]),
        copy_in(factors.at[0], f_buf.at[0], sems.at[1]),
        copy_in(spatial.at[1], s_buf, sems.at[2]),
    ]
    loads[0].wait()
    after = diagonal(scales[1:2, :]) + dot_hi(f_buf[1], f_buf[1], NT)
    loads[1].wait()
    before = diagonal(scales[0:1, :]) + dot_hi(f_buf[0], f_buf[0], NT)
    loads[2].wait()
    square = diagonal(damping[1:2, :]) + spatial_gain * dot_hi(s_buf[...], s_buf[...], NT) + after + before
    e_buf[0:N, :] = before
    e_buf[N:TALL, :] = jnp.where(flag[0] > 0, after, 0.0)
    saves = [copy_in(e_buf, edges, sems.at[3])]
    inverse = newton_inverse(square)
    w_buf[...] = inverse
    saves.append(copy_in(w_buf, root, sems.at[4]))
    vector = jnp.broadcast_to(source[1:2, :], (8, N))
    z = dot_hi(vector, inverse)
    local[...] = z
    after = e_buf[N:TALL, :]
    right = dot_hi(after, inverse)
    r_buf[...] = right
    saves.append(copy_in(r_buf, stack.at[pl.ds(N, N)], sems.at[5]))
    pack(m_buf, after - dot_hi(right, after, NT), dot_hi(z, after, NT))
    saves.append(copy_in(m_buf, message, sems.at[6]))
    pack(p_buf, square, vector)
    saves.append(copy_in(p_buf, packed, sems.at[7]))
    for save in saves:
        save.wait()


def first_link_kernel(flag, root, edges, stack_in, stack, link, w_buf, e_buf, t_buf, r_buf, l_buf, sems):
    loads = [
        copy_in(root, w_buf, sems.at[0]),
        copy_in(edges, e_buf, sems.at[1]),
        copy_in(stack_in.at[pl.ds(N, N)], r_buf, sems.at[2]),
    ]
    loads[0].wait()
    loads[1].wait()
    left = dot_hi(e_buf[0:N, :], w_buf[...])
    t_buf[...] = left
    save = copy_in(t_buf, stack.at[pl.ds(0, N)], sems.at[3])
    loads[2].wait()
    odd = flag[0] > 0
    l_buf[...] = dot_hi(
        jnp.where(odd, r_buf[...], left), jnp.where(odd, e_buf[0:N, :], e_buf[N:TALL, :]), NT
    )
    last = copy_in(l_buf, link, sems.at[4])
    save.wait()
    last.wait()


def first_own_kernel(damping, source, local, spatial, edges, stack, state, s_buf, e_buf, t_buf, p_buf, sems):
    loads = [
        copy_in(spatial.at[0], s_buf, sems.at[0]),
        copy_in(edges.at[pl.ds(0, N)], e_buf, sems.at[1]),
        copy_in(stack.at[pl.ds(0, N)], t_buf, sems.at[2]),
    ]
    for load in loads:
        load.wait()
    before = e_buf[...]
    square = diagonal(damping[0:1, :]) + spatial_gain * dot_hi(s_buf[...], s_buf[...], NT) + before
    vector = jnp.broadcast_to(source[0:1, :], (8, N)) + dot_hi(local[...], before, NT)
    pack(p_buf, square - dot_hi(t_buf[...], before, NT), vector)
    save = copy_in(p_buf, state, sems.at[3])
    save.wait()


def invert_kernel(flag, state, left, right, logs, kept, prior, new_state, inverse, local, bufs, w_buf, sems):
    loads = [
        copy_in(state, bufs.at[0], sems.at[0]),
        copy_in(left, bufs.at[1], sems.at[1]),
        copy_in(right, bufs.at[2], sems.at[2]),
    ]
    for load in loads:
        load.wait()
    bufs[0] = bufs[0] + bufs[1] + bufs[2]
    save = copy_in(bufs.at[0], new_state, sems.at[3])
    local[...] = prior[...]

    @pl.when(flag[0] > 0)
    def _():
        inv = newton_inverse(unpack(bufs.at[0]))
        w_buf[...] = inv
        keep = copy_in(w_buf, inverse, sems.at[4])
        local[...] = dot_hi(unpack_vector(bufs.at[0]), inv)
        keep.wait()

    save.wait()


def product_kernel(flag, local, inverse, near, far, prior, stack, left, right, w_buf, n_buf, t_buf, m_buf, sems):
    @pl.when(flag[0] > 0)
    def _():
        loads = [
            copy_in(inverse, w_buf, sems.at[0]),
            copy_in(near, n_buf.at[0], sems.at[1]),
            copy_in(far, n_buf.at[1], sems.at[2]),
        ]
        z = local[...]
        loads[0].wait()
        saves = []
        for k, out in enumerate((left, right)):
            loads[k + 1].wait()
            part = dot_hi(n_buf[k], w_buf[...])
            t_buf[k] = part
            saves.append(copy_in(t_buf.at[k], stack.at[pl.ds(k * N, N)], sems.at[3 + 2 * k]))
            pack(m_buf.at[k], -dot_hi(part, n_buf[k], NT), dot_hi(z, n_buf[k], NT))
            saves.append(copy_in(m_buf.at[k], out, sems.at[4 + 2 * k]))
        for save in saves:
            save.wait()


def link_kernel(flag, side, stack, near, far, link, t_buf, n_buf, l_buf, sems):
    @pl.when(flag[0] > 0)
    def _():
        @pl.when(side[0] > 0)
        def _():
            pltpu.make_async_copy(stack.at[pl.ds(N, N)], t_buf, sems.at[0]).start()
            pltpu.make_async_copy(near, n_buf, sems.at[1]).start()

        @pl.when(side[0] == 0)
        def _():
            pltpu.make_async_copy(stack.at[pl.ds(0, N)], t_buf, sems.at[0]).start()
            pltpu.make_async_copy(far, n_buf, sems.at[1]).start()

        pltpu.make_async_copy(near, t_buf, sems.at[0]).wait()
        pltpu.make_async_copy(near, n_buf, sems.at[1]).wait()
        l_buf[...] = dot_hi(t_buf[...], n_buf[...], NT)
        save = copy_in(l_buf, link, sems.at[2])
        save.wait()


def log_kernel(flag, packed, inverse, after, prior, logs, a_buf, w_buf, sems):
    logs[...] = prior[...]

    @pl.when(flag[0] > 0)
    def _():
        loads = [
            copy_in(packed.at[pl.ds(k * B, B)], a_buf.at[pl.ds(i * B, B), pl.ds(j * B, B)], sems.at[k])
            for k, (i, j) in enumerate(BLOCKS[:3])
        ]
        loads.append(copy_in(inverse.at[pl.ds(2 * B, B), pl.ds(2 * B, B)], w_buf, sems.at[3]))
        for load in loads:
            load.wait()
        a_buf[0:B, B : 2 * B] = a_buf[B : 2 * B, 0:B].T
        logs[...] = prior[...] + log_det_ratio(a_buf[...], w_buf[...])


def descend_kernel(flag, local, left, right, current, stack, value, s_buf, sems):
    value[...] = current[...]

    @pl.when(flag[0] > 0)
    def _():
        load = copy_in(stack, s_buf, sems.at[0])
        both = jnp.concatenate([left[...], right[...]], axis=1)
        load.wait()
        value[...] = local[...] + dot_hi(both, s_buf[...])


SMEM = pl.BlockSpec(memory_space=pltpu.SMEM)
VMEM = pl.BlockSpec(memory_space=pltpu.VMEM)
ANY = pl.BlockSpec(memory_space=pltpu.HBM)


def shape(*dims):
    return jax.ShapeDtypeStruct(dims, f32)


def buf(*dims):
    return pltpu.VMEM(dims, f32)


def call(kernel, name, micros, ins, outs, scratch, sems, args, aliases={}):
    return pl.pallas_call(
        kernel,
        name=name,
        out_shape=[o[1] for o in outs],
        in_specs=ins,
        out_specs=[o[0] for o in outs],
        scratch_shapes=scratch + [pltpu.SemaphoreType.DMA((sems,))],
        input_output_aliases=aliases,
        cost_estimate=pl.CostEstimate(
            flops=int(micros * 1.0e9), bytes_accessed=int(micros * 3.0e6), transcendentals=0
        ),
        compiler_params=pltpu.CompilerParams(vmem_limit_bytes=VMEM_LIMIT),
    )(*args)


PACKED = (ANY, shape(ROWS, B))
SQUARE = (ANY, shape(N, N))
TWO = (ANY, shape(TALL, N))
VECTOR = (VMEM, shape(8, N))


def local(damping, spatial_factor, edge_scale, edge_factor, forcing):
    size = lax.axis_size("tm")
    position = lax.axis_index("tm")

    def flag(condition):
        return jnp.reshape(condition.astype(jnp.int32), (1,))

    def send(x, pairs):
        return lax.ppermute(x, "tm", [p for p in pairs if 0 <= p[1] < size])

    def log_of(condition, packed, inverse, after, logs):
        (logs,) = call(
            log_kernel, "log", 0.2, [SMEM, ANY, ANY, ANY, VMEM], [(VMEM, shape(8, B))],
            [buf(2 * B, 2 * B), buf(B, B)], 4,
            (flag(condition), packed, inverse, after, logs), {4: 0},
        )
        return logs

    def invert(condition, state, left, right, logs, inverse, own):
        return call(
            invert_kernel, "invert", 6, [SMEM] + [ANY] * 5 + [VMEM], [PACKED, SQUARE, VECTOR],
            [buf(3, ROWS, B), buf(N, N)], 5,
            (flag(condition), state, left, right, logs, inverse, own), {5: 1, 6: 2},
        )

    message, root, edges, stack1, local1, packed = call(
        first_kernel, "first", 11, [SMEM] + [VMEM] * 3 + [ANY] * 2,
        [PACKED, SQUARE, TWO, TWO, VECTOR, PACKED],
        [buf(N, N), buf(2, N, N), buf(TALL, N), buf(N, N), buf(N, N), buf(ROWS, B), buf(ROWS, B)], 8,
        (flag(position < size - 1), damping, edge_scale, forcing, spatial_factor, edge_factor),
    )
    from_left = send(message, [(i, i + 1) for i in range(size)])
    stack1, link = call(
        first_link_kernel, "first_link", 4, [SMEM] + [ANY] * 3, [TWO, SQUARE],
        [buf(N, N), buf(TALL, N), buf(N, N), buf(N, N), buf(N, N)], 5,
        (flag(position % 2 == 1), root, edges, stack1), {3: 0},
    )
    near = send(link, [(i, i + 1) for i in range(0, size, 2)])
    far = link
    (state,) = call(
        first_own_kernel, "first_own", 4, [VMEM] * 3 + [ANY] * 3, [PACKED],
        [buf(N, N), buf(N, N), buf(N, N), buf(ROWS, B)], 4,
        (damping, forcing, local1, spatial_factor, edges, stack1),
    )
    logs = jnp.zeros((8, B), f32)
    stack = jnp.zeros((TALL, N), f32)
    inverse = jnp.zeros((N, N), f32)
    own = jnp.zeros((8, N), f32)
    nothing = jnp.zeros((ROWS, B), f32)
    from_right = nothing
    logs_done = logs
    span = 1
    while span < size:
        step = 2 * span
        active = position % step == span
        state, inverse, own = invert(active, state, from_left, from_right, logs_done, inverse, own)
        stack, to_left, to_right = call(
            product_kernel, "product", 6, [SMEM, VMEM] + [ANY] * 4, [TWO, PACKED, PACKED],
            [buf(N, N), buf(2, N, N), buf(2, N, N), buf(2, ROWS, B)], 7,
            (flag(active), own, inverse, near, far, stack), {5: 0},
        )
        odd = range(span, size, step)
        back = [(i, i - span) for i in odd]
        from_right = send(to_left, back)
        if step < size:
            from_left = send(to_right, [(i, i + span) for i in odd])
            side = (position // step) % 2 == 1
            (link,) = call(
                link_kernel, "link", 3, [SMEM] * 2 + [ANY] * 3, [SQUARE],
                [buf(N, N), buf(N, N), buf(N, N)], 3,
                (flag(active), flag(side), stack, near, far),
            )
            near = send(link, [(i, i + span) for i in odd if (i // step) % 2 == 0])
            far = send(link, [(i, i - span) for i in odd if (i // step) % 2 == 1])
        else:
            from_left = nothing
        if span == 1:
            logs = log_of(position >= 0, packed, root, stack, logs)
        logs_done = log_of(active, state, inverse, stack, logs)
        logs = logs_done + send(logs_done, back)
        span = step
    state, inverse, own = invert(position == 0, state, from_left, from_right, logs_done, inverse, own)
    value = jnp.where(position == 0, own, 0.0)
    logs = log_of(position == 0, state, inverse, own, logs)
    log_row = jnp.where(position == 0, logs, 0.0)

    def descend(condition, own, left, right, current, stack):
        (value,) = call(
            descend_kernel, "descend", 1, [SMEM] + [VMEM] * 4 + [ANY], [VECTOR], [buf(TALL, N)], 1,
            (flag(condition), own, left, right, current, stack), {4: 0},
        )
        return value

    zero = jnp.zeros((8, N), f32)
    span = size
    while span > 1:
        step = span
        span //= 2
        odd = range(span, size, step)
        right = [(i + span, i) for i in odd if i + span < size]
        left_value = send(value, [(i - span, i) for i in odd])
        right_value = send(value, right) if right else zero
        log_row = log_row + send(log_row, [(i - span, i) for i in odd])
        value = descend(position % step == span, own, left_value, right_value, value, stack)
    right_value = send(value, [(i + 1, i) for i in range(size - 1)])
    second = descend(position >= 0, local1, value, right_value, zero, stack1)
    solution = jnp.concatenate([value[0:1], second[0:1]], axis=0)
    logdet_mean = log_row[0, 0:1] / (size * 2 * N)
    return (solution, logdet_mean)


def solution(mesh):
    return jax.shard_map(
        local,
        mesh=mesh,
        in_specs=(
            P(("hyp", "tm"), None),
            P(("hyp", "tm"), None, None),
            P(("hyp", "tm"), None),
            P(("hyp", "tm"), None, None),
            P(("hyp", "tm"), None),
        ),
        out_specs=(P(("hyp", "tm"), None), P("hyp")),
        check_vma=False,
    )
```

```python
import functools

import jax
import jax.numpy as jnp
from jax import lax
from jax.experimental import pallas as pl
from jax.experimental.pallas import tpu as pltpu
from jax.sharding import PartitionSpec as P

N = 384
B = 128
spatial_gain = 0.02
f32 = jnp.float32
bf16 = jnp.bfloat16
NN = (((1,), (0,)), ((), ()))
NT = (((1,), (1,)), ((), ()))
BLOCKS = ((0, 0), (1, 0), (1, 1), (2, 0), (2, 1), (2, 2))
ROWS = 6 * B + 24
TALL = 2 * N
VMEM_LIMIT = 24 << 20
LOG_COEFS = (0.999973924, -0.499286916, 0.326642792, -0.219344301, 0.120321356, -0.037876697, 0.002717324)


def split3(x):
    top, rest = split2_wide(x)
    middle, last = split2_wide(rest)
    return top, middle, last.astype(bf16)


def split2_wide(x):
    top = x.astype(bf16)
    return top, x - top.astype(f32)


def dot_hi(a, b, dims=NN):
    a1, a2, a3 = split3(a)
    b1, b2, b3 = split3(b)
    return lax.dot_general(
        jnp.concatenate([a1, a1, a2, a2, a1, a3], axis=1),
        jnp.concatenate([b1, b2, b1, b2, b3, b1], axis=dims[0][1][0]),
        dims,
        preferred_element_type=f32,
    )


def dot_one(a, b):
    return jnp.dot(a.astype(bf16), b.astype(bf16), preferred_element_type=f32)


def split2(x):
    top = x.astype(bf16)
    return top, (x - top.astype(f32)).astype(bf16)


def dot_three(a, b):
    a1, a2 = split2(a)
    b1, b2 = split2(b)
    return jnp.dot(
        jnp.concatenate([a1, a1, a2], axis=1),
        jnp.concatenate([b1, b2, b1], axis=0),
        preferred_element_type=f32,
    )


def eye_mask(n=N):
    return lax.broadcasted_iota(jnp.int32, (n, n), 0) == lax.broadcasted_iota(jnp.int32, (n, n), 1)


def total(x):
    return jnp.sum(x)


def unpack(ref):
    blocks = {}
    for k, (i, j) in enumerate(BLOCKS):
        block = ref[k * B : (k + 1) * B, :]
        blocks[i, j] = block
        if i != j:
            blocks[j, i] = block.T
    return jnp.concatenate(
        [jnp.concatenate([blocks[i, j] for j in range(3)], axis=1) for i in range(3)], axis=0
    )


def unpack_vector(ref):
    return jnp.concatenate([ref[6 * B + 8 * k : 6 * B + 8 * k + 8, :] for k in range(3)], axis=1)


def pack(ref, square, vector):
    for k, (i, j) in enumerate(BLOCKS):
        ref[k * B : (k + 1) * B, :] = square[i * B : (i + 1) * B, j * B : (j + 1) * B]
    for k in range(3):
        ref[6 * B + 8 * k : 6 * B + 8 * k + 8, :] = vector[:, k * B : (k + 1) * B]


def newton_inverse(a):
    eye = eye_mask()
    diag_col = jnp.sum(jnp.where(eye, a, 0.0), axis=1, keepdims=True)
    diag_row = jnp.sum(jnp.where(eye, a, 0.0), axis=0, keepdims=True)
    inv_col = 1.0 / diag_col
    inv_row = 1.0 / diag_row
    high = jnp.max(jnp.sum(jnp.abs(a), axis=1, keepdims=True) * inv_col)
    ratio = 10.0
    width = 1.0 - 1.0 / ratio
    centre = (1.0 + 1.0 / ratio) / width
    bound = 1.0 / (2.0 * centre * centre - 1.0)
    alpha = 8.0 * centre * bound / (width * high)
    beta = -8.0 * bound / (width * width * high * high)
    x = beta * (inv_col * a * inv_row) + jnp.where(eye, alpha * inv_row, 0.0)
    one = jnp.where(eye, 1.0, 0.0)
    a_low = a.astype(bf16)
    for _ in range(2):
        half = 0.5 * bound * bound
        gain = 1.0 / (1.0 - half)
        bound = half * gain
        r = one - jnp.dot(a_low, x.astype(bf16), preferred_element_type=f32)
        x = gain * (x + dot_one(x, r))
    r = one - dot_three(a, x)
    x = x + dot_one(x, r)

    def more(carry):
        return jnp.logical_and(carry[1] > 1e-5, carry[0] < 40)

    def step(carry):
        count, _, x = carry
        r = jnp.where(eye_mask(), 1.0, 0.0) - dot_hi(a, x)
        return count + 1, total(r * r), x + dot_three(x, r)

    return lax.while_loop(more, step, (jnp.int32(0), jnp.float32(1.0), x))[2]


def log_start(a):
    n = a.shape[0]
    eye = eye_mask(n)
    diag_col = jnp.sum(jnp.where(eye, a, 0.0), axis=1, keepdims=True)
    diag_row = jnp.sum(jnp.where(eye, a, 0.0), axis=0, keepdims=True)
    scaled = lax.rsqrt(diag_col) * a * lax.rsqrt(diag_row)
    high = jnp.max(jnp.sum(jnp.abs(scaled), axis=1, keepdims=True))
    base = total(jnp.log(diag_row)) + n * jnp.max(jnp.log(jnp.full((8, B), high)))
    return base, jnp.where(eye, 1.0, 0.0) - scaled * (1.0 / high)


def log_terms(r, r2, r4):
    c1, c2, c3, c4, c5, c6, c8 = LOG_COEFS
    terms = r * (c2 * r + c3 * r2 + c5 * r4) + r2 * (c4 * r2 + c6 * r4) + c8 * (r4 * r4)
    return total(terms + c1 * jnp.where(eye_mask(r.shape[0]), r, 0.0))


def trace(r):
    return total(jnp.where(eye_mask(r.shape[0]), r, 0.0))


def log_det_ratio(tops, bottoms):
    signs = [1.0] * len(tops) + [-1.0] * len(bottoms)
    bases, rs = zip(*[log_start(a) for a in tops + bottoms])

    def more(carry):
        return jnp.logical_and(carry[1] > 1e-4, carry[0] < 40)

    def step(carry):
        count, _, value, rs, squares = carry
        fourths = tuple(dot_hi(r2, r2) for r2 in squares)
        for sign, r, r2, r4 in zip(signs, rs, squares, fourths):
            value = value + sign * log_terms(r, r2, r4)
        most = trace(squares[0])
        for r2 in squares[1:]:
            most = jnp.maximum(most, trace(r2))
        return count + 1, most, value, squares, fourths

    carry = (jnp.int32(0), jnp.float32(1.0), jnp.float32(0.0), tuple(rs), tuple(dot_hi(r, r) for r in rs))
    _, _, value, rs, _ = lax.while_loop(more, step, carry)
    for sign, base, r in zip(signs, bases, rs):
        value = value + sign * (trace(r) - base)
    return -value


def row_of(row):
    return jnp.where(lax.broadcasted_iota(jnp.int32, (8, N), 0) == 0, row, 0.0)


def diagonal(row):
    return jnp.where(eye_mask(), row, 0.0)


def edge_kernel(scales, factors, edges):
    for k in range(2):
        edges[k * N : (k + 1) * N, :] = diagonal(scales[k : k + 1, :]) + dot_hi(factors[k], factors[k], NT)


def keep_for_log(square, inverse, block, corner):
    block[...] = square[0 : 2 * B, 0 : 2 * B]
    corner[...] = inverse[2 * B :, 2 * B :]


def first_kernel(size, pos, damping, source, spatial, edges, message, root, edges_out, fold, local, block, corner):
    before = edges[0:N, :]
    after = edges[N:TALL, :]
    square = diagonal(damping[1:2, :]) + spatial_gain * dot_hi(spatial[1], spatial[1], NT) + after + before
    after = jnp.where(pos[0] < size - 1, after, 0.0)
    edges_out[0:N, :] = before
    edges_out[N:TALL, :] = after
    inverse = newton_inverse(square)
    keep_for_log(square, inverse, block, corner)
    root[...] = inverse
    z = dot_hi(row_of(source[1:2, :]), inverse)
    local[...] = z
    after = edges_out[N:TALL, :]
    right = dot_hi(after, inverse)
    fold[...] = right
    pack(message, after - dot_hi(right, after, NT), dot_hi(z, after, NT))


def second_kernel(
    pos, damping, source, spatial, root, edges, fold, local,
    stack, link, state, own_stack, own, block, corner,
):
    for empty in (own_stack, own, block, corner):
        empty[...] = jnp.zeros(empty.shape, f32)
    before = edges[0:N, :]
    left = dot_hi(before, root[...])
    stack[0:N, :] = left
    stack[N:TALL, :] = fold[...]
    odd = pos[0] % 2 == 1
    link[...] = dot_hi(jnp.where(odd, fold[...], left), jnp.where(odd, before, edges[N:TALL, :]), NT)
    square = diagonal(damping[0:1, :]) + spatial_gain * dot_hi(spatial[0], spatial[0], NT) + before
    vector = row_of(source[0:1, :]) + dot_hi(local[...], before, NT)
    pack(state, square - dot_hi(stack[0:N, :], before, NT), vector)


def invert_kernel(test, pos, state, prior, prior_block, prior_corner, after, *rest):
    *received, new_state, inverse, local, block, corner = rest
    new_state[...] = sum([r[...] for r in received], state[...])

    @pl.when(test(pos[0]))
    def _():
        square = unpack(new_state)
        inv = newton_inverse(square)
        inverse[...] = inv
        keep_for_log(square, inv, block, corner)
        local[...] = dot_hi(unpack_vector(new_state), inv)

    @pl.when(jnp.logical_not(test(pos[0])))
    def _():
        local[...] = prior[...]
        block[...] = prior_block[...]
        corner[...] = prior_corner[...]


def product_kernel(test, side, pos, local, inverse, near, far, prior, stack, left, right, one, other):
    @pl.when(test(pos[0]))
    def _():
        z = local[...]
        parts = []
        for k, (edge, out) in enumerate(((near, left), (far, right))):
            part = dot_hi(edge[...], inverse[...])
            stack[k * N : (k + 1) * N, :] = part
            pack(out, -dot_hi(part, edge[...], NT), dot_hi(z, edge[...], NT))
        up = side(pos[0])
        one[...] = jnp.where(up, stack[N:TALL, :], stack[0:N, :])
        other[...] = jnp.where(up, near[...], far[...])

    @pl.when(jnp.logical_not(test(pos[0])))
    def _():
        stack[...] = prior[...]


def link_kernel(test, pos, one, other, link):
    @pl.when(test(pos[0]))
    def _():
        link[...] = dot_hi(one[...], other[...], NT)


def last_kernel(test, pos, local, inverse, near, other, prior, stack, state):
    @pl.when(test(pos[0]))
    def _():
        part = dot_hi(near[...], inverse[...])
        stack[0:N, :] = part
        stack[N:TALL, :] = jnp.zeros((N, N), f32)
        pack(state, -dot_hi(part, near[...], NT), dot_hi(local[...], near[...], NT))
        state[...] = state[...] + other[...]

    @pl.when(jnp.logical_not(test(pos[0])))
    def _():
        stack[...] = prior[...]


def root_kernel(test, pos, state, block, corner, value):
    @pl.when(test(pos[0]))
    def _():
        square = unpack(state)
        inv = newton_inverse(square)
        keep_for_log(square, inv, block, corner)
        value[...] = dot_hi(unpack_vector(state), inv)


def log_kernel(test, pairs, pos, after, *rest):
    *refs, logs = rest
    tops, bottoms, came = refs[:pairs], refs[pairs : 2 * pairs], refs[2 * pairs :]
    logs[...] = sum([c[...] for c in came], jnp.zeros((8, B), f32))
    if pairs:

        @pl.when(test(pos[0]))
        def _():
            logs[...] = logs[...] + log_det_ratio([t[...] for t in tops], [b[...] for b in bottoms])


def descend_kernel(test, pos, local, left, current, stack, *rest):
    *right, value = rest

    @pl.when(test(pos[0]))
    def _():
        both = left[...]
        part = stack[0:N, :]
        if right:
            both = jnp.concatenate([left[...], right[0][...]], axis=1)
            part = stack[...]
        found = local[...] + dot_hi(both, part)
        value[...] = jnp.where(log_rows(), left[...], found)

    @pl.when(jnp.logical_not(test(pos[0])))
    def _():
        value[...] = current[...]


def log_rows():
    return lax.broadcasted_iota(jnp.int32, (8, N), 0) == 1


def join_kernel(value, logs, joined):
    joined[...] = jnp.where(log_rows(), jnp.concatenate([logs[0:1, :]] * 3, axis=1), value[...])


def top_kernel(test, pos, local, first, stack, both):
    @pl.when(test(pos[0]))
    def _():
        found = local[...] + dot_hi(first[...], stack[0:N, :])
        both[0:8, :] = jnp.where(log_rows(), first[...], found)
        both[8:16, :] = first[...]

    @pl.when(jnp.logical_not(test(pos[0])))
    def _():
        both[...] = jnp.zeros((16, N), f32)


def second_value_kernel(half, pos, both, came, value):
    value[...] = jnp.where(pos[0] == half, both[0:8, :], jnp.where(pos[0] == 0, came[...], 0.0))


def descend_both_kernel(test, pos, local, both, left, current, stack, value):
    test_first, test_any = test
    first = test_first(pos[0])
    near = jnp.where(first, both[8:16, :], left[...])
    far = jnp.where(first, both[0:8, :], 0.0)
    found = local[...] + dot_hi(jnp.concatenate([near, far], axis=1), stack[...])
    value[...] = jnp.where(test_any(pos[0]), jnp.where(log_rows(), near, found), current[...])


def output_kernel(scale, local, left, right, stack, solution, logs):
    both = jnp.concatenate([left[...], right[...]], axis=1)
    second = local[...] + dot_hi(both, stack[...])
    solution[0:1, :] = left[0:1, :]
    solution[1:2, :] = second[0:1, :]
    logs[...] = left[...] * scale


SMEM = pl.BlockSpec(memory_space=pltpu.SMEM)
VMEM = pl.BlockSpec(memory_space=pltpu.VMEM)
ANY = pl.BlockSpec(memory_space=pl.ANY)


def shape(*dims):
    return jax.ShapeDtypeStruct(dims, f32)


def call(kernel, name, micros, specs, outs, args, aliases={}):
    return pl.pallas_call(
        kernel,
        name=name,
        out_shape=outs,
        in_specs=specs,
        out_specs=[VMEM] * len(outs),
        input_output_aliases=aliases,
        cost_estimate=pl.CostEstimate(
            flops=int(micros * 1.0e9), bytes_accessed=int(micros * 3.0e6), transcendentals=0
        ),
        compiler_params=pltpu.CompilerParams(vmem_limit_bytes=VMEM_LIMIT),
    )(*args)


PACKED = shape(ROWS, B)
SQUARE = shape(N, N)
TWO = shape(TALL, N)
VECTOR = shape(8, N)
BLOCK = shape(2 * B, 2 * B)
CORNER = shape(B, B)


def local(damping, spatial_factor, edge_scale, edge_factor, forcing):
    size = lax.axis_size("tm")
    half = size // 2
    pos = jnp.reshape(lax.axis_index("tm").astype(jnp.int32), (1,))

    def send(x, pairs):
        return lax.ppermute(x, "tm", [p for p in pairs if 0 <= p[1] < size])

    def odd_of(span):
        return lambda p: p % (2 * span) == span

    def log_of(test, pairs, after, *args):
        (logs,) = call(
            functools.partial(log_kernel, test, pairs), "log", 0.2, [SMEM, ANY] + [VMEM] * len(args),
            [shape(8, B)], (pos, after) + args,
        )
        return logs

    (edges,) = call(edge_kernel, "edges", 3, [VMEM] * 2, [TWO], (edge_scale, edge_factor))
    message, root, edges, fold, local1, block1, corner1 = call(
        functools.partial(first_kernel, size), "first", 9, [SMEM] + [VMEM] * 4,
        [PACKED, SQUARE, TWO, SQUARE, VECTOR, BLOCK, CORNER],
        (pos, damping, forcing, spatial_factor, edges),
    )
    received = [send(message, [(i, i + 1) for i in range(size)])]
    stack1, link, state, stack, own, block, corner = call(
        second_kernel, "second", 5, [SMEM] + [VMEM] * 7, [TWO, SQUARE, PACKED, TWO, VECTOR, BLOCK, CORNER],
        (pos, damping, forcing, spatial_factor, root, edges, fold, local1),
    )
    near = send(link, [(i, i + 1) for i in range(0, size, 2)])
    far = link
    after = block1
    span = 1
    while span < size:
        step = 2 * span
        active = odd_of(span)
        state, inverse, own, block, corner = call(
            functools.partial(invert_kernel, active), "invert", 6,
            [SMEM] + [VMEM] * 4 + [ANY] + [VMEM] * len(received), [PACKED, SQUARE, VECTOR, BLOCK, CORNER],
            (pos, state, own, block, corner, after, *received), {2: 2, 3: 3, 4: 4},
        )
        odd = range(span, size, step)
        back = [(i, i - span) for i in odd]
        if step < size:
            stack, to_left, to_right, one, other = call(
                functools.partial(product_kernel, active, lambda p, step=step: (p // step) % 2 == 1),
                "product", 6, [SMEM] + [VMEM] * 5, [TWO, PACKED, PACKED, SQUARE, SQUARE],
                (pos, own, inverse, near, far, stack), {5: 0},
            )
            received = [send(to_left, back), send(to_right, [(i, i + span) for i in odd])]
            (link,) = call(
                functools.partial(link_kernel, active), "link", 3, [SMEM] + [VMEM] * 2, [SQUARE],
                (pos, one, other),
            )
            near = send(link, [(i, i + span) for i in odd if (i // step) % 2 == 0])
            far = send(link, [(i, i - span) for i in odd if (i // step) % 2 == 1])
        else:
            other = send(state, [(0, half)])
            stack, last = call(
                functools.partial(last_kernel, active), "last", 6, [SMEM] + [VMEM] * 5, [TWO, PACKED],
                (pos, own, inverse, near, other, stack), {5: 0},
            )
        if span == 1:
            after = log_of(lambda p: p >= 0, 1, one, block1, corner1)
            logs = [after]
        else:
            before = span // 2
            after = log_of(odd_of(before), 1, one if step < size else inverse, block, corner, *logs)
            logs = [after, send(after, [(i, i - before) for i in range(before, size, span)])]
        span = step
    at_half = odd_of(half)
    last_block, last_corner, first_value = call(
        functools.partial(root_kernel, at_half), "root", 6, [SMEM, VMEM], [BLOCK, CORNER, VECTOR], (pos, last),
    )
    total_logs = log_of(None, 0, last, *logs)
    came = send(total_logs, [(0, half)])
    logs = log_of(at_half, 2, last, block, last_block, corner, last_corner, total_logs, came)
    (first_value,) = call(join_kernel, "join", 0.2, [VMEM] * 2, [VECTOR], (first_value, logs))
    (both,) = call(
        functools.partial(top_kernel, at_half), "top", 1, [SMEM] + [VMEM] * 3, [shape(16, N)],
        (pos, own, first_value, stack),
    )
    came = send(first_value, [(half, 0)])
    (value,) = call(
        functools.partial(second_value_kernel, half), "value", 0.2, [SMEM] + [VMEM] * 2, [VECTOR], (pos, both, came)
    )
    span = half
    while span > 1:
        step = span
        span //= 2
        odd = range(span, size, step)
        left_value = send(value, [(i - span, i) for i in odd])
        if step == half:
            both = send(both, [(half, span)])
            tests = (lambda p, span=span: p == span, odd_of(span))
            (value,) = call(
                functools.partial(descend_both_kernel, tests), "descend", 1, [SMEM] + [VMEM] * 5, [VECTOR],
                (pos, own, both, left_value, value, stack),
            )
        else:
            right_value = send(value, [(i + span, i) for i in odd if i + span < size])
            (value,) = call(
                functools.partial(descend_kernel, odd_of(span)), "descend", 1, [SMEM] + [VMEM] * 5, [VECTOR],
                (pos, own, left_value, value, stack, right_value),
            )
    right_value = send(value, [(i + 1, i) for i in range(size - 1)])
    solution, logs = call(
        functools.partial(output_kernel, 1.0 / (size * 2 * N)), "output", 1, [VMEM] * 4, [shape(2, N), VECTOR],
        (local1, value, right_value, stack1),
    )
    return (solution, logs[1, 0:1])


def solution(mesh):
    return jax.shard_map(
        local,
        mesh=mesh,
        in_specs=(
            P(("hyp", "tm"), None),
            P(("hyp", "tm"), None, None),
            P(("hyp", "tm"), None),
            P(("hyp", "tm"), None, None),
            P(("hyp", "tm"), None),
        ),
        out_specs=(P(("hyp", "tm"), None), P("hyp")),
        check_vma=False,
    )
```

```python
import functools

import jax
import jax.numpy as jnp
from jax import lax
from jax.experimental import pallas as pl
from jax.experimental.pallas import tpu as pltpu
from jax.sharding import PartitionSpec as P

N = 384
B = 128
spatial_gain = 0.02
f32 = jnp.float32
bf16 = jnp.bfloat16
NN = (((1,), (0,)), ((), ()))
NT = (((1,), (1,)), ((), ()))
BLOCKS = ((0, 0), (1, 0), (1, 1), (2, 0), (2, 1), (2, 2))
ROWS = 6 * B + 24
TALL = 2 * N
VMEM_LIMIT = 24 << 20
LOG_COEFS = (0.999973924, -0.499286916, 0.326642792, -0.219344301, 0.120321356, -0.037876697, 0.002717324)


def split3(x):
    top, rest = split2_wide(x)
    middle, last = split2_wide(rest)
    return top, middle, last.astype(bf16)


def split2_wide(x):
    top = x.astype(bf16)
    return top, x - top.astype(f32)


def dot_hi(a, b, dims=NN):
    a1, a2, a3 = split3(a)
    b1, b2, b3 = split3(b)
    return lax.dot_general(
        jnp.concatenate([a1, a1, a2, a2, a1, a3], axis=1),
        jnp.concatenate([b1, b2, b1, b2, b3, b1], axis=dims[0][1][0]),
        dims,
        preferred_element_type=f32,
    )


def dot_one(a, b):
    return jnp.dot(a.astype(bf16), b.astype(bf16), preferred_element_type=f32)


def split2(x):
    top = x.astype(bf16)
    return top, (x - top.astype(f32)).astype(bf16)


def dot_three(a, b):
    a1, a2 = split2(a)
    b1, b2 = split2(b)
    return jnp.dot(
        jnp.concatenate([a1, a1, a2], axis=1),
        jnp.concatenate([b1, b2, b1], axis=0),
        preferred_element_type=f32,
    )


def eye_mask(n=N):
    return lax.broadcasted_iota(jnp.int32, (n, n), 0) == lax.broadcasted_iota(jnp.int32, (n, n), 1)


def total(x):
    return jnp.sum(x)


def unpack(ref):
    blocks = {}
    for k, (i, j) in enumerate(BLOCKS):
        block = ref[k * B : (k + 1) * B, :]
        blocks[i, j] = block
        if i != j:
            blocks[j, i] = block.T
    return jnp.concatenate(
        [jnp.concatenate([blocks[i, j] for j in range(3)], axis=1) for i in range(3)], axis=0
    )


def unpack_vector(ref):
    return jnp.concatenate([ref[6 * B + 8 * k : 6 * B + 8 * k + 8, :] for k in range(3)], axis=1)


def pack(ref, square, vector):
    for k, (i, j) in enumerate(BLOCKS):
        ref[k * B : (k + 1) * B, :] = square[i * B : (i + 1) * B, j * B : (j + 1) * B]
    for k in range(3):
        ref[6 * B + 8 * k : 6 * B + 8 * k + 8, :] = vector[:, k * B : (k + 1) * B]


def newton_inverse(a):
    eye = eye_mask()
    diag_col = jnp.sum(jnp.where(eye, a, 0.0), axis=1, keepdims=True)
    diag_row = jnp.sum(jnp.where(eye, a, 0.0), axis=0, keepdims=True)
    inv_col = 1.0 / diag_col
    inv_row = 1.0 / diag_row
    high = jnp.max(jnp.sum(jnp.abs(a), axis=1, keepdims=True) * inv_col)
    ratio = 10.0
    width = 1.0 - 1.0 / ratio
    centre = (1.0 + 1.0 / ratio) / width
    bound = 1.0 / (2.0 * centre * centre - 1.0)
    alpha = 8.0 * centre * bound / (width * high)
    beta = -8.0 * bound / (width * width * high * high)
    x = beta * (inv_col * a * inv_row) + jnp.where(eye, alpha * inv_row, 0.0)
    one = jnp.where(eye, 1.0, 0.0)
    a_low = a.astype(bf16)
    for _ in range(2):
        half = 0.5 * bound * bound
        gain = 1.0 / (1.0 - half)
        bound = half * gain
        r = one - jnp.dot(a_low, x.astype(bf16), preferred_element_type=f32)
        x = gain * (x + dot_one(x, r))
    r = one - dot_three(a, x)
    x = x + dot_one(x, r)

    def more(carry):
        return jnp.logical_and(carry[1] > 1e-5, carry[0] < 40)

    def step(carry):
        count, _, x = carry
        r = jnp.where(eye_mask(), 1.0, 0.0) - dot_hi(a, x)
        return count + 1, total(r * r), x + dot_three(x, r)

    return lax.while_loop(more, step, (jnp.int32(0), jnp.float32(1.0), x))[2]


def log_start(a):
    n = a.shape[0]
    eye = eye_mask(n)
    diag_col = jnp.sum(jnp.where(eye, a, 0.0), axis=1, keepdims=True)
    diag_row = jnp.sum(jnp.where(eye, a, 0.0), axis=0, keepdims=True)
    scaled = lax.rsqrt(diag_col) * a * lax.rsqrt(diag_row)
    high = jnp.max(jnp.sum(jnp.abs(scaled), axis=1, keepdims=True))
    base = total(jnp.log(diag_row)) + n * jnp.max(jnp.log(jnp.full((8, B), high)))
    return base, jnp.where(eye, 1.0, 0.0) - scaled * (1.0 / high)


def log_terms(r, r2, r4):
    c1, c2, c3, c4, c5, c6, c8 = LOG_COEFS
    terms = r * (c2 * r + c3 * r2 + c5 * r4) + r2 * (c4 * r2 + c6 * r4) + c8 * (r4 * r4)
    return total(terms + c1 * jnp.where(eye_mask(r.shape[0]), r, 0.0))


def trace(r):
    return total(jnp.where(eye_mask(r.shape[0]), r, 0.0))


def log_det_ratio(tops, bottoms):
    signs = [1.0] * len(tops) + [-1.0] * len(bottoms)
    bases, rs = zip(*[log_start(a) for a in tops + bottoms])

    def more(carry):
        return jnp.logical_and(carry[1] > 1e-4, carry[0] < 40)

    def step(carry):
        count, _, value, rs, squares = carry
        fourths = tuple(dot_hi(r2, r2) for r2 in squares)
        for sign, r, r2, r4 in zip(signs, rs, squares, fourths):
            value = value + sign * log_terms(r, r2, r4)
        most = trace(squares[0])
        for r2 in squares[1:]:
            most = jnp.maximum(most, trace(r2))
        return count + 1, most, value, squares, fourths

    carry = (jnp.int32(0), jnp.float32(1.0), jnp.float32(0.0), tuple(rs), tuple(dot_hi(r, r) for r in rs))
    _, _, value, rs, _ = lax.while_loop(more, step, carry)
    for sign, base, r in zip(signs, bases, rs):
        value = value + sign * (trace(r) - base)
    return -value


def row_of(row):
    return jnp.where(lax.broadcasted_iota(jnp.int32, (8, N), 0) == 0, row, 0.0)


def diagonal(row):
    return jnp.where(eye_mask(), row, 0.0)


def edge_kernel(scales, factors, edges):
    for k in range(2):
        edges[k * N : (k + 1) * N, :] = diagonal(scales[k : k + 1, :]) + dot_hi(factors[k], factors[k], NT)


def keep_for_log(square, inverse, block, corner):
    block[...] = square[0 : 2 * B, 0 : 2 * B]
    corner[...] = inverse[2 * B :, 2 * B :]


def first_kernel(size, pos, damping, source, spatial, edges, message, root, edges_out, fold, local, block, corner):
    before = edges[0:N, :]
    after = edges[N:TALL, :]
    square = diagonal(damping[1:2, :]) + spatial_gain * dot_hi(spatial[1], spatial[1], NT) + after + before
    after = jnp.where(pos[0] < size - 1, after, 0.0)
    edges_out[0:N, :] = before
    edges_out[N:TALL, :] = after
    inverse = newton_inverse(square)
    keep_for_log(square, inverse, block, corner)
    root[...] = inverse
    z = dot_hi(row_of(source[1:2, :]), inverse)
    local[...] = z
    after = edges_out[N:TALL, :]
    right = dot_hi(after, inverse)
    fold[...] = right
    pack(message, after - dot_hi(right, after, NT), dot_hi(z, after, NT))


def second_kernel(
    pos, damping, source, spatial, root, edges, fold, local,
    stack, link, state, own_stack, own, block, corner,
):
    for empty in (own_stack, own, block, corner):
        empty[...] = jnp.zeros(empty.shape, f32)
    before = edges[0:N, :]
    left = dot_hi(before, root[...])
    stack[0:N, :] = left
    stack[N:TALL, :] = fold[...]
    odd = pos[0] % 2 == 1
    link[...] = dot_hi(jnp.where(odd, fold[...], left), jnp.where(odd, before, edges[N:TALL, :]), NT)
    square = diagonal(damping[0:1, :]) + spatial_gain * dot_hi(spatial[0], spatial[0], NT) + before
    vector = row_of(source[0:1, :]) + dot_hi(local[...], before, NT)
    pack(state, square - dot_hi(stack[0:N, :], before, NT), vector)


def invert_kernel(test, pos, state, prior, prior_block, prior_corner, after, *rest):
    *received, new_state, inverse, local, block, corner = rest
    new_state[...] = sum([r[...] for r in received], state[...])

    @pl.when(test(pos[0]))
    def _():
        square = unpack(new_state)
        inv = newton_inverse(square)
        inverse[...] = inv
        keep_for_log(square, inv, block, corner)
        local[...] = dot_hi(unpack_vector(new_state), inv)

    @pl.when(jnp.logical_not(test(pos[0])))
    def _():
        local[...] = prior[...]
        block[...] = prior_block[...]
        corner[...] = prior_corner[...]


def product_kernel(test, side, pos, local, inverse, near, far, prior, stack, left, right, one, other):
    @pl.when(test(pos[0]))
    def _():
        z = local[...]
        parts = []
        for k, (edge, out) in enumerate(((near, left), (far, right))):
            part = dot_hi(edge[...], inverse[...])
            stack[k * N : (k + 1) * N, :] = part
            pack(out, -dot_hi(part, edge[...], NT), dot_hi(z, edge[...], NT))
        up = side(pos[0])
        one[...] = jnp.where(up, stack[N:TALL, :], stack[0:N, :])
        other[...] = jnp.where(up, near[...], far[...])

    @pl.when(jnp.logical_not(test(pos[0])))
    def _():
        stack[...] = prior[...]


def link_kernel(test, pos, one, other, link):
    @pl.when(test(pos[0]))
    def _():
        link[...] = dot_hi(one[...], other[...], NT)


def forward_kernel(message, after, out):
    out[...] = message[...]


def last_kernel(test, pos, local, inverse, near, other, prior, stack, state):
    @pl.when(test(pos[0]))
    def _():
        part = dot_hi(near[...], inverse[...])
        stack[0:N, :] = part
        stack[N:TALL, :] = jnp.zeros((N, N), f32)
        pack(state, -dot_hi(part, near[...], NT), dot_hi(local[...], near[...], NT))
        state[...] = state[...] + other[...]

    @pl.when(jnp.logical_not(test(pos[0])))
    def _():
        stack[...] = prior[...]


def root_kernel(test, pos, state, block, corner, value):
    @pl.when(test(pos[0]))
    def _():
        square = unpack(state)
        inv = newton_inverse(square)
        keep_for_log(square, inv, block, corner)
        value[...] = dot_hi(unpack_vector(state), inv)


def log_kernel(test, pairs, pos, after, *rest):
    *refs, logs = rest
    tops, bottoms, came = refs[:pairs], refs[pairs : 2 * pairs], refs[2 * pairs :]
    logs[...] = sum([c[...] for c in came], jnp.zeros((8, B), f32))
    if pairs:

        @pl.when(test(pos[0]))
        def _():
            logs[...] = logs[...] + log_det_ratio([t[...] for t in tops], [b[...] for b in bottoms])


def descend_kernel(test, pos, local, left, current, stack, *rest):
    *right, value = rest

    @pl.when(test(pos[0]))
    def _():
        both = left[...]
        part = stack[0:N, :]
        if right:
            both = jnp.concatenate([left[...], right[0][...]], axis=1)
            part = stack[...]
        found = local[...] + dot_hi(both, part)
        value[...] = jnp.where(log_rows(), left[...], found)

    @pl.when(jnp.logical_not(test(pos[0])))
    def _():
        value[...] = current[...]


def log_rows():
    return lax.broadcasted_iota(jnp.int32, (8, N), 0) == 1


def join_kernel(value, logs, joined):
    joined[...] = jnp.where(log_rows(), jnp.concatenate([logs[0:1, :]] * 3, axis=1), value[...])


def top_kernel(test, pos, local, first, stack, both):
    @pl.when(test(pos[0]))
    def _():
        found = local[...] + dot_hi(first[...], stack[0:N, :])
        both[0:8, :] = jnp.where(log_rows(), first[...], found)
        both[8:16, :] = first[...]

    @pl.when(jnp.logical_not(test(pos[0])))
    def _():
        both[...] = jnp.zeros((16, N), f32)


def second_value_kernel(half, pos, both, came, value):
    value[...] = jnp.where(pos[0] == half, both[0:8, :], jnp.where(pos[0] == 0, came[...], 0.0))


def descend_both_kernel(test, pos, local, both, left, current, stack, value):
    test_first, test_any = test
    first = test_first(pos[0])
    near = jnp.where(first, both[8:16, :], left[...])
    far = jnp.where(first, both[0:8, :], 0.0)
    found = local[...] + dot_hi(jnp.concatenate([near, far], axis=1), stack[...])
    value[...] = jnp.where(test_any(pos[0]), jnp.where(log_rows(), near, found), current[...])


def output_kernel(scale, local, left, right, stack, solution, logs):
    both = jnp.concatenate([left[...], right[...]], axis=1)
    second = local[...] + dot_hi(both, stack[...])
    solution[0:1, :] = left[0:1, :]
    solution[1:2, :] = second[0:1, :]
    logs[...] = left[...] * scale


SMEM = pl.BlockSpec(memory_space=pltpu.SMEM)
VMEM = pl.BlockSpec(memory_space=pltpu.VMEM)
ANY = pl.BlockSpec(memory_space=pl.ANY)


def shape(*dims):
    return jax.ShapeDtypeStruct(dims, f32)


def call(kernel, name, micros, specs, outs, args, aliases={}):
    return pl.pallas_call(
        kernel,
        name=name,
        out_shape=outs,
        in_specs=specs,
        out_specs=[VMEM] * len(outs),
        input_output_aliases=aliases,
        cost_estimate=pl.CostEstimate(
            flops=int(micros * 1.0e9), bytes_accessed=int(micros * 3.0e6), transcendentals=0
        ),
        compiler_params=pltpu.CompilerParams(vmem_limit_bytes=VMEM_LIMIT),
    )(*args)


PACKED = shape(ROWS, B)
SQUARE = shape(N, N)
TWO = shape(TALL, N)
VECTOR = shape(8, N)
BLOCK = shape(2 * B, 2 * B)
CORNER = shape(B, B)


def local(damping, spatial_factor, edge_scale, edge_factor, forcing):
    size = lax.axis_size("tm")
    half = size // 2
    pos = jnp.reshape(lax.axis_index("tm").astype(jnp.int32), (1,))

    def send(x, pairs):
        return lax.ppermute(x, "tm", [p for p in pairs if 0 <= p[1] < size])

    def odd_of(span):
        return lambda p: p % (2 * span) == span

    def ways(span):
        if span == 0:
            return []
        odd = range(span, size, 2 * span)
        if span in (2, 8):
            return [[(i, i - span // 2) for i in odd], [(i - span // 2, i - span) for i in odd]]
        return [[(i, i - span) for i in odd]]

    def follow(x, hops):
        for hop in hops:
            x = send(x, hop)
        return x

    def log_of(test, pairs, after, *args):
        (logs,) = call(
            functools.partial(log_kernel, test, pairs), "log", 0.2, [SMEM, ANY] + [VMEM] * len(args),
            [shape(8, B)], (pos, after) + args,
        )
        return logs

    (edges,) = call(edge_kernel, "edges", 3, [VMEM] * 2, [TWO], (edge_scale, edge_factor))
    message, root, edges, fold, local1, block1, corner1 = call(
        functools.partial(first_kernel, size), "first", 9, [SMEM] + [VMEM] * 4,
        [PACKED, SQUARE, TWO, SQUARE, VECTOR, BLOCK, CORNER],
        (pos, damping, forcing, spatial_factor, edges),
    )
    received = [send(message, [(i, i + 1) for i in range(size)])]
    stack1, link, state, stack, own, block, corner = call(
        second_kernel, "second", 5, [SMEM] + [VMEM] * 7, [TWO, SQUARE, PACKED, TWO, VECTOR, BLOCK, CORNER],
        (pos, damping, forcing, spatial_factor, root, edges, fold, local1),
    )
    near = send(link, [(i, i + 1) for i in range(0, size, 2)])
    far = link
    after = block1
    span = 1
    while span < size:
        step = 2 * span
        active = odd_of(span)
        state, inverse, own, block, corner = call(
            functools.partial(invert_kernel, active), "invert", 1 if len(ways(span // 2)) == 2 else 6,
            [SMEM] + [VMEM] * 4 + [ANY] + [VMEM] * len(received), [PACKED, SQUARE, VECTOR, BLOCK, CORNER],
            (pos, state, own, block, corner, after, *received), {2: 2, 3: 3, 4: 4},
        )
        odd = range(span, size, step)
        if step < size:
            stack, to_left, to_right, one, other = call(
                functools.partial(product_kernel, active, lambda p, step=step: (p // step) % 2 == 1),
                "product", 6, [SMEM] + [VMEM] * 5, [TWO, PACKED, PACKED, SQUARE, SQUARE],
                (pos, own, inverse, near, far, stack), {5: 0},
            )
            left_ways = ways(span)
            between = send(to_left, left_ways[0])
            received = [between, send(to_right, [(i, i + span) for i in odd])]
            (link,) = call(
                functools.partial(link_kernel, active), "link", 3, [SMEM] + [VMEM] * 2, [SQUARE],
                (pos, one, other),
            )
            if len(left_ways) == 2:
                (between,) = call(forward_kernel, "forward", 0.2, [VMEM, ANY], [PACKED], (between, link))
                received[0] = send(between, left_ways[1])
            near = send(link, [(i, i + span) for i in odd if (i // step) % 2 == 0])
            far = send(link, [(i, i - span) for i in odd if (i // step) % 2 == 1])
        else:
            other = send(state, [(0, half)])
            stack, last = call(
                functools.partial(last_kernel, active), "last", 6, [SMEM] + [VMEM] * 5, [TWO, PACKED],
                (pos, own, inverse, near, other, stack), {5: 0},
            )
        if span == 1:
            after = log_of(lambda p: p >= 0, 1, one, block1, corner1)
            logs = [after]
        else:
            before = span // 2
            after = log_of(odd_of(before), 1, between if step < size else inverse, block, corner, *logs)
            logs = [after, follow(after, ways(before))]
        span = step
    at_half = odd_of(half)
    last_block, last_corner, first_value = call(
        functools.partial(root_kernel, at_half), "root", 6, [SMEM, VMEM], [BLOCK, CORNER, VECTOR], (pos, last),
    )
    total_logs = log_of(None, 0, last, *logs)
    came = send(total_logs, [(0, half)])
    logs = log_of(at_half, 2, last, block, last_block, corner, last_corner, total_logs, came)
    (first_value,) = call(join_kernel, "join", 0.2, [VMEM] * 2, [VECTOR], (first_value, logs))
    (both,) = call(
        functools.partial(top_kernel, at_half), "top", 1, [SMEM] + [VMEM] * 3, [shape(16, N)],
        (pos, own, first_value, stack),
    )
    came = send(first_value, [(half, 0)])
    (value,) = call(
        functools.partial(second_value_kernel, half), "value", 0.2, [SMEM] + [VMEM] * 2, [VECTOR], (pos, both, came)
    )
    span = half
    while span > 1:
        step = span
        span //= 2
        odd = range(span, size, step)
        left_value = send(value, [(i - span, i) for i in odd])
        if step == half:
            both = send(both, [(half, span)])
            tests = (lambda p, span=span: p == span, odd_of(span))
            (value,) = call(
                functools.partial(descend_both_kernel, tests), "descend", 1, [SMEM] + [VMEM] * 5, [VECTOR],
                (pos, own, both, left_value, value, stack),
            )
        else:
            right_value = send(value, [(i + span, i) for i in odd if i + span < size])
            (value,) = call(
                functools.partial(descend_kernel, odd_of(span)), "descend", 1, [SMEM] + [VMEM] * 5, [VECTOR],
                (pos, own, left_value, value, stack, right_value),
            )
    right_value = send(value, [(i + 1, i) for i in range(size - 1)])
    solution, logs = call(
        functools.partial(output_kernel, 1.0 / (size * 2 * N)), "output", 1, [VMEM] * 4, [shape(2, N), VECTOR],
        (local1, value, right_value, stack1),
    )
    return (solution, logs[1, 0:1])


def solution(mesh):
    return jax.shard_map(
        local,
        mesh=mesh,
        in_specs=(
            P(("hyp", "tm"), None),
            P(("hyp", "tm"), None, None),
            P(("hyp", "tm"), None),
            P(("hyp", "tm"), None, None),
            P(("hyp", "tm"), None),
        ),
        out_specs=(P(("hyp", "tm"), None), P("hyp")),
        check_vma=False,
    )
```

```python
import functools

import jax
import jax.numpy as jnp
from jax import lax
from jax.experimental import pallas as pl
from jax.experimental.pallas import tpu as pltpu
from jax.sharding import PartitionSpec as P

N = 384
B = 128
spatial_gain = 0.02
f32 = jnp.float32
bf16 = jnp.bfloat16
NN = (((1,), (0,)), ((), ()))
NT = (((1,), (1,)), ((), ()))
BLOCKS = ((0, 0), (1, 0), (1, 1), (2, 0), (2, 1), (2, 2))
ROWS = 6 * B + 24
TALL = 2 * N
VMEM_LIMIT = 24 << 20
LOG_COEFS = (0.999973924, -0.499286916, 0.326642792, -0.219344301, 0.120321356, -0.037876697, 0.002717324)


def split3(x):
    top, rest = split2_wide(x)
    middle, last = split2_wide(rest)
    return top, middle, last.astype(bf16)


def split2_wide(x):
    top = x.astype(bf16)
    return top, x - top.astype(f32)


def dot_hi(a, b, dims=NN):
    a1, a2, a3 = split3(a)
    b1, b2, b3 = split3(b)
    return lax.dot_general(
        jnp.concatenate([a1, a1, a2, a2, a1, a3], axis=1),
        jnp.concatenate([b1, b2, b1, b2, b3, b1], axis=dims[0][1][0]),
        dims,
        preferred_element_type=f32,
    )


def dot_one(a, b):
    return jnp.dot(a.astype(bf16), b.astype(bf16), preferred_element_type=f32)


def split2(x):
    top = x.astype(bf16)
    return top, (x - top.astype(f32)).astype(bf16)


def dot_three(a, b, dims=NN):
    a1, a2 = split2(a)
    b1, b2 = split2(b)
    return lax.dot_general(
        jnp.concatenate([a1, a1, a2], axis=1),
        jnp.concatenate([b1, b2, b1], axis=dims[0][1][0]),
        dims,
        preferred_element_type=f32,
    )


def eye_mask(n=N):
    return lax.broadcasted_iota(jnp.int32, (n, n), 0) == lax.broadcasted_iota(jnp.int32, (n, n), 1)


def total(x):
    return jnp.sum(x)


def unpack(ref):
    blocks = {}
    for k, (i, j) in enumerate(BLOCKS):
        block = ref[k * B : (k + 1) * B, :]
        blocks[i, j] = block
        if i != j:
            blocks[j, i] = block.T
    return jnp.concatenate(
        [jnp.concatenate([blocks[i, j] for j in range(3)], axis=1) for i in range(3)], axis=0
    )


def unpack_vector(ref):
    return jnp.concatenate([ref[6 * B + 8 * k : 6 * B + 8 * k + 8, :] for k in range(3)], axis=1)


def pack(ref, square, vector):
    for k, (i, j) in enumerate(BLOCKS):
        ref[k * B : (k + 1) * B, :] = square[i * B : (i + 1) * B, j * B : (j + 1) * B]
    for k in range(3):
        ref[6 * B + 8 * k : 6 * B + 8 * k + 8, :] = vector[:, k * B : (k + 1) * B]


def newton_inverse(a):
    eye = eye_mask()
    diag_col = jnp.sum(jnp.where(eye, a, 0.0), axis=1, keepdims=True)
    diag_row = jnp.sum(jnp.where(eye, a, 0.0), axis=0, keepdims=True)
    inv_col = 1.0 / diag_col
    inv_row = 1.0 / diag_row
    high = jnp.max(jnp.sum(jnp.abs(a), axis=1, keepdims=True) * inv_col)
    ratio = 10.0
    width = 1.0 - 1.0 / ratio
    centre = (1.0 + 1.0 / ratio) / width
    bound = 1.0 / (2.0 * centre * centre - 1.0)
    alpha = 8.0 * centre * bound / (width * high)
    beta = -8.0 * bound / (width * width * high * high)
    x = beta * (inv_col * a * inv_row) + jnp.where(eye, alpha * inv_row, 0.0)
    one = jnp.where(eye, 1.0, 0.0)
    a_low = a.astype(bf16)
    for _ in range(2):
        half = 0.5 * bound * bound
        gain = 1.0 / (1.0 - half)
        bound = half * gain
        r = one - jnp.dot(a_low, x.astype(bf16), preferred_element_type=f32)
        x = gain * (x + dot_one(x, r))
    r = one - dot_three(a, x)
    x = x + dot_one(x, r)

    def more(carry):
        return jnp.logical_and(carry[1] > 1e-5, carry[0] < 40)

    def step(carry):
        count, _, x = carry
        r = jnp.where(eye_mask(), 1.0, 0.0) - dot_hi(a, x)
        return count + 1, total(r * r), x + dot_three(x, r)

    return lax.while_loop(more, step, (jnp.int32(0), jnp.float32(1.0), x))[2]


def log_start(a):
    n = a.shape[0]
    eye = eye_mask(n)
    diag_col = jnp.sum(jnp.where(eye, a, 0.0), axis=1, keepdims=True)
    diag_row = jnp.sum(jnp.where(eye, a, 0.0), axis=0, keepdims=True)
    scaled = lax.rsqrt(diag_col) * a * lax.rsqrt(diag_row)
    high = jnp.max(jnp.sum(jnp.abs(scaled), axis=1, keepdims=True))
    base = total(jnp.log(diag_row)) + n * jnp.max(jnp.log(jnp.full((8, B), high)))
    return base, jnp.where(eye, 1.0, 0.0) - scaled * (1.0 / high)


def log_terms(r, r2, r4):
    c1, c2, c3, c4, c5, c6, c8 = LOG_COEFS
    terms = r * (c2 * r + c3 * r2 + c5 * r4) + r2 * (c4 * r2 + c6 * r4) + c8 * (r4 * r4)
    return total(terms + c1 * jnp.where(eye_mask(r.shape[0]), r, 0.0))


def trace(r):
    return total(jnp.where(eye_mask(r.shape[0]), r, 0.0))


def log_det_ratio(tops, bottoms):
    signs = [1.0] * len(tops) + [-1.0] * len(bottoms)
    bases, rs = zip(*[log_start(a) for a in tops + bottoms])

    def more(carry):
        return jnp.logical_and(carry[1] > 1e-4, carry[0] < 40)

    def step(carry):
        count, _, value, rs, squares = carry
        fourths = tuple(dot_hi(r2, r2) for r2 in squares)
        for sign, r, r2, r4 in zip(signs, rs, squares, fourths):
            value = value + sign * log_terms(r, r2, r4)
        most = trace(squares[0])
        for r2 in squares[1:]:
            most = jnp.maximum(most, trace(r2))
        return count + 1, most, value, squares, fourths

    carry = (jnp.int32(0), jnp.float32(1.0), jnp.float32(0.0), tuple(rs), tuple(dot_hi(r, r) for r in rs))
    _, _, value, rs, _ = lax.while_loop(more, step, carry)
    for sign, base, r in zip(signs, bases, rs):
        value = value + sign * (trace(r) - base)
    return -value


def row_of(row):
    return jnp.where(lax.broadcasted_iota(jnp.int32, (8, N), 0) == 0, row, 0.0)


def diagonal(row):
    return jnp.where(eye_mask(), row, 0.0)


def edge_kernel(scales, factors, edges):
    for k in range(2):
        edges[k * N : (k + 1) * N, :] = diagonal(scales[k : k + 1, :]) + dot_hi(factors[k], factors[k], NT)


def keep_for_log(square, inverse, block, corner):
    block[...] = square[0 : 2 * B, 0 : 2 * B]
    corner[...] = inverse[2 * B :, 2 * B :]


def first_kernel(size, pos, damping, source, spatial, edges, message, root, edges_out, fold, local, block, corner):
    before = edges[0:N, :]
    after = edges[N:TALL, :]
    square = diagonal(damping[1:2, :]) + spatial_gain * dot_hi(spatial[1], spatial[1], NT) + after + before
    after = jnp.where(pos[0] < size - 1, after, 0.0)
    edges_out[0:N, :] = before
    edges_out[N:TALL, :] = after
    inverse = newton_inverse(square)
    keep_for_log(square, inverse, block, corner)
    root[...] = inverse
    z = dot_hi(row_of(source[1:2, :]), inverse)
    local[...] = z
    after = edges_out[N:TALL, :]
    right = dot_hi(after, inverse)
    fold[...] = right
    pack(message, after - dot_hi(right, after, NT), dot_hi(z, after, NT))


def second_kernel(
    pos, damping, source, spatial, root, edges, fold, local,
    stack, link, state, own_stack, own, block, corner,
):
    for empty in (own_stack, own, block, corner):
        empty[...] = jnp.zeros(empty.shape, f32)
    before = edges[0:N, :]
    left = dot_hi(before, root[...])
    stack[0:N, :] = left
    stack[N:TALL, :] = fold[...]
    odd = pos[0] % 2 == 1
    link[...] = dot_hi(jnp.where(odd, fold[...], left), jnp.where(odd, before, edges[N:TALL, :]), NT)
    square = diagonal(damping[0:1, :]) + spatial_gain * dot_hi(spatial[0], spatial[0], NT) + before
    vector = row_of(source[0:1, :]) + dot_hi(local[...], before, NT)
    pack(state, square - dot_hi(stack[0:N, :], before, NT), vector)


def invert_kernel(test, pos, state, prior, prior_block, prior_corner, after, *rest):
    *received, new_state, inverse, local, block, corner = rest
    new_state[...] = sum([r[...] for r in received], state[...])

    @pl.when(test(pos[0]))
    def _():
        square = unpack(new_state)
        inv = newton_inverse(square)
        inverse[...] = inv
        keep_for_log(square, inv, block, corner)
        local[...] = dot_hi(unpack_vector(new_state), inv)

    @pl.when(jnp.logical_not(test(pos[0])))
    def _():
        local[...] = prior[...]
        block[...] = prior_block[...]
        corner[...] = prior_corner[...]


def product_kernel(test, side, pos, local, inverse, near, far, prior, stack, left, right, one, other):
    @pl.when(test(pos[0]))
    def _():
        z = local[...]
        parts = []
        for k, (edge, out) in enumerate(((near, left), (far, right))):
            part = dot_three(edge[...], inverse[...])
            stack[k * N : (k + 1) * N, :] = part
            pack(out, -dot_three(part, edge[...], NT), dot_three(z, edge[...], NT))
        up = side(pos[0])
        one[...] = jnp.where(up, stack[N:TALL, :], stack[0:N, :])
        other[...] = jnp.where(up, near[...], far[...])

    @pl.when(jnp.logical_not(test(pos[0])))
    def _():
        stack[...] = prior[...]


def link_kernel(test, pos, one, other, link):
    @pl.when(test(pos[0]))
    def _():
        link[...] = dot_three(one[...], other[...], NT)


def forward_kernel(message, after, out):
    out[...] = message[...]


def last_kernel(test, pos, local, inverse, near, other, prior, stack, state):
    @pl.when(test(pos[0]))
    def _():
        part = dot_three(near[...], inverse[...])
        stack[0:N, :] = part
        stack[N:TALL, :] = jnp.zeros((N, N), f32)
        pack(state, -dot_three(part, near[...], NT), dot_three(local[...], near[...], NT))
        state[...] = state[...] + other[...]

    @pl.when(jnp.logical_not(test(pos[0])))
    def _():
        stack[...] = prior[...]


def root_kernel(test, pos, state, block, corner, value):
    @pl.when(test(pos[0]))
    def _():
        square = unpack(state)
        inv = newton_inverse(square)
        keep_for_log(square, inv, block, corner)
        value[...] = dot_hi(unpack_vector(state), inv)


def log_kernel(test, pairs, pos, after, *rest):
    *refs, logs = rest
    tops, bottoms, came = refs[:pairs], refs[pairs : 2 * pairs], refs[2 * pairs :]
    logs[...] = sum([c[...] for c in came], jnp.zeros((8, B), f32))
    if pairs:

        @pl.when(test(pos[0]))
        def _():
            logs[...] = logs[...] + log_det_ratio([t[...] for t in tops], [b[...] for b in bottoms])


def descend_kernel(test, pos, local, left, current, stack, *rest):
    *right, value = rest

    @pl.when(test(pos[0]))
    def _():
        both = left[...]
        part = stack[0:N, :]
        if right:
            both = jnp.concatenate([left[...], right[0][...]], axis=1)
            part = stack[...]
        found = local[...] + dot_hi(both, part)
        value[...] = jnp.where(log_rows(), left[...], found)

    @pl.when(jnp.logical_not(test(pos[0])))
    def _():
        value[...] = current[...]


def log_rows():
    return lax.broadcasted_iota(jnp.int32, (8, N), 0) == 1


def join_kernel(value, logs, joined):
    joined[...] = jnp.where(log_rows(), jnp.concatenate([logs[0:1, :]] * 3, axis=1), value[...])


def top_kernel(test, pos, local, first, stack, both):
    @pl.when(test(pos[0]))
    def _():
        found = local[...] + dot_hi(first[...], stack[0:N, :])
        both[0:8, :] = jnp.where(log_rows(), first[...], found)
        both[8:16, :] = first[...]

    @pl.when(jnp.logical_not(test(pos[0])))
    def _():
        both[...] = jnp.zeros((16, N), f32)


def second_value_kernel(half, pos, both, came, value):
    value[...] = jnp.where(pos[0] == half, both[0:8, :], jnp.where(pos[0] == 0, came[...], 0.0))


def descend_both_kernel(test, pos, local, both, left, current, stack, value):
    test_first, test_any = test
    first = test_first(pos[0])
    near = jnp.where(first, both[8:16, :], left[...])
    far = jnp.where(first, both[0:8, :], 0.0)
    found = local[...] + dot_hi(jnp.concatenate([near, far], axis=1), stack[...])
    value[...] = jnp.where(test_any(pos[0]), jnp.where(log_rows(), near, found), current[...])


def output_kernel(scale, local, left, right, stack, solution, logs):
    both = jnp.concatenate([left[...], right[...]], axis=1)
    second = local[...] + dot_hi(both, stack[...])
    solution[0:1, :] = left[0:1, :]
    solution[1:2, :] = second[0:1, :]
    logs[...] = left[...] * scale


SMEM = pl.BlockSpec(memory_space=pltpu.SMEM)
VMEM = pl.BlockSpec(memory_space=pltpu.VMEM)
ANY = pl.BlockSpec(memory_space=pl.ANY)


def shape(*dims):
    return jax.ShapeDtypeStruct(dims, f32)


def call(kernel, name, micros, specs, outs, args, aliases={}):
    return pl.pallas_call(
        kernel,
        name=name,
        out_shape=outs,
        in_specs=specs,
        out_specs=[VMEM] * len(outs),
        input_output_aliases=aliases,
        cost_estimate=pl.CostEstimate(
            flops=int(micros * 1.0e9), bytes_accessed=int(micros * 3.0e6), transcendentals=0
        ),
        compiler_params=pltpu.CompilerParams(vmem_limit_bytes=VMEM_LIMIT),
    )(*args)


PACKED = shape(ROWS, B)
SQUARE = shape(N, N)
TWO = shape(TALL, N)
VECTOR = shape(8, N)
BLOCK = shape(2 * B, 2 * B)
CORNER = shape(B, B)


def local(damping, spatial_factor, edge_scale, edge_factor, forcing):
    size = lax.axis_size("tm")
    half = size // 2
    pos = jnp.reshape(lax.axis_index("tm").astype(jnp.int32), (1,))

    def send(x, pairs):
        return lax.ppermute(x, "tm", [p for p in pairs if 0 <= p[1] < size])

    def odd_of(span):
        return lambda p: p % (2 * span) == span

    def ways(span):
        if span == 0:
            return []
        odd = range(span, size, 2 * span)
        if span in (2, 8):
            return [[(i, i - span // 2) for i in odd], [(i - span // 2, i - span) for i in odd]]
        return [[(i, i - span) for i in odd]]

    def follow(x, hops):
        for hop in hops:
            x = send(x, hop)
        return x

    def log_of(test, pairs, after, *args):
        (logs,) = call(
            functools.partial(log_kernel, test, pairs), "log", 0.2, [SMEM, ANY] + [VMEM] * len(args),
            [shape(8, B)], (pos, after) + args,
        )
        return logs

    (edges,) = call(edge_kernel, "edges", 3, [VMEM] * 2, [TWO], (edge_scale, edge_factor))
    message, root, edges, fold, local1, block1, corner1 = call(
        functools.partial(first_kernel, size), "first", 9, [SMEM] + [VMEM] * 4,
        [PACKED, SQUARE, TWO, SQUARE, VECTOR, BLOCK, CORNER],
        (pos, damping, forcing, spatial_factor, edges),
    )
    received = [send(message, [(i, i + 1) for i in range(size)])]
    stack1, link, state, stack, own, block, corner = call(
        second_kernel, "second", 5, [SMEM] + [VMEM] * 7, [TWO, SQUARE, PACKED, TWO, VECTOR, BLOCK, CORNER],
        (pos, damping, forcing, spatial_factor, root, edges, fold, local1),
    )
    near = send(link, [(i, i + 1) for i in range(0, size, 2)])
    far = link
    after = block1
    span = 1
    while span < size:
        step = 2 * span
        active = odd_of(span)
        state, inverse, own, block, corner = call(
            functools.partial(invert_kernel, active), "invert", 1 if len(ways(span // 2)) == 2 else 6,
            [SMEM] + [VMEM] * 4 + [ANY] + [VMEM] * len(received), [PACKED, SQUARE, VECTOR, BLOCK, CORNER],
            (pos, state, own, block, corner, after, *received), {2: 2, 3: 3, 4: 4},
        )
        odd = range(span, size, step)
        if step < size:
            stack, to_left, to_right, one, other = call(
                functools.partial(product_kernel, active, lambda p, step=step: (p // step) % 2 == 1),
                "product", 6, [SMEM] + [VMEM] * 5, [TWO, PACKED, PACKED, SQUARE, SQUARE],
                (pos, own, inverse, near, far, stack), {5: 0},
            )
            left_ways = ways(span)
            between = send(to_left, left_ways[0])
            received = [between, send(to_right, [(i, i + span) for i in odd])]
            (link,) = call(
                functools.partial(link_kernel, active), "link", 3, [SMEM] + [VMEM] * 2, [SQUARE],
                (pos, one, other),
            )
            if len(left_ways) == 2:
                (between,) = call(forward_kernel, "forward", 0.2, [VMEM, ANY], [PACKED], (between, link))
                received[0] = send(between, left_ways[1])
            near = send(link, [(i, i + span) for i in odd if (i // step) % 2 == 0])
            far = send(link, [(i, i - span) for i in odd if (i // step) % 2 == 1])
        else:
            other = send(state, [(0, half)])
            stack, last = call(
                functools.partial(last_kernel, active), "last", 6, [SMEM] + [VMEM] * 5, [TWO, PACKED],
                (pos, own, inverse, near, other, stack), {5: 0},
            )
        if span == 1:
            after = log_of(lambda p: p >= 0, 1, one, block1, corner1)
            logs = [after]
        else:
            before = span // 2
            after = log_of(odd_of(before), 1, between if step < size else inverse, block, corner, *logs)
            logs = [after, follow(after, ways(before))]
        span = step
    at_half = odd_of(half)
    last_block, last_corner, first_value = call(
        functools.partial(root_kernel, at_half), "root", 6, [SMEM, VMEM], [BLOCK, CORNER, VECTOR], (pos, last),
    )
    total_logs = log_of(None, 0, last, *logs)
    came = send(total_logs, [(0, half)])
    logs = log_of(at_half, 2, last, block, last_block, corner, last_corner, total_logs, came)
    (first_value,) = call(join_kernel, "join", 0.2, [VMEM] * 2, [VECTOR], (first_value, logs))
    (both,) = call(
        functools.partial(top_kernel, at_half), "top", 1, [SMEM] + [VMEM] * 3, [shape(16, N)],
        (pos, own, first_value, stack),
    )
    came = send(first_value, [(half, 0)])
    (value,) = call(
        functools.partial(second_value_kernel, half), "value", 0.2, [SMEM] + [VMEM] * 2, [VECTOR], (pos, both, came)
    )
    span = half
    while span > 1:
        step = span
        span //= 2
        odd = range(span, size, step)
        left_value = send(value, [(i - span, i) for i in odd])
        if step == half:
            both = send(both, [(half, span)])
            tests = (lambda p, span=span: p == span, odd_of(span))
            (value,) = call(
                functools.partial(descend_both_kernel, tests), "descend", 1, [SMEM] + [VMEM] * 5, [VECTOR],
                (pos, own, both, left_value, value, stack),
            )
        else:
            right_value = send(value, [(i + span, i) for i in odd if i + span < size])
            (value,) = call(
                functools.partial(descend_kernel, odd_of(span)), "descend", 1, [SMEM] + [VMEM] * 5, [VECTOR],
                (pos, own, left_value, value, stack, right_value),
            )
    right_value = send(value, [(i + 1, i) for i in range(size - 1)])
    solution, logs = call(
        functools.partial(output_kernel, 1.0 / (size * 2 * N)), "output", 1, [VMEM] * 4, [shape(2, N), VECTOR],
        (local1, value, right_value, stack1),
    )
    return (solution, logs[1, 0:1])


def solution(mesh):
    return jax.shard_map(
        local,
        mesh=mesh,
        in_specs=(
            P(("hyp", "tm"), None),
            P(("hyp", "tm"), None, None),
            P(("hyp", "tm"), None),
            P(("hyp", "tm"), None, None),
            P(("hyp", "tm"), None),
        ),
        out_specs=(P(("hyp", "tm"), None), P("hyp")),
        check_vma=False,
    )
```

```python
import functools

import jax
import jax.numpy as jnp
from jax import lax
from jax.experimental import pallas as pl
from jax.experimental.pallas import tpu as pltpu
from jax.sharding import PartitionSpec as P

N = 384
B = 128
spatial_gain = 0.02
f32 = jnp.float32
bf16 = jnp.bfloat16
NN = (((1,), (0,)), ((), ()))
NT = (((1,), (1,)), ((), ()))
BLOCKS = ((0, 0), (1, 0), (1, 1), (2, 0), (2, 1), (2, 2))
ROWS = 6 * B + 24
TALL = 2 * N
VMEM_LIMIT = 24 << 20
LOG_COEFS = (0.999973924, -0.499286916, 0.326642792, -0.219344301, 0.120321356, -0.037876697, 0.002717324)


def split3(x):
    top, rest = split2_wide(x)
    middle, last = split2_wide(rest)
    return top, middle, last.astype(bf16)


def split2_wide(x):
    top = x.astype(bf16)
    return top, x - top.astype(f32)


def dot_hi(a, b, dims=NN):
    a1, a2, a3 = split3(a)
    b1, b2, b3 = split3(b)
    return lax.dot_general(
        jnp.concatenate([a1, a1, a2, a2, a1, a3], axis=1),
        jnp.concatenate([b1, b2, b1, b2, b3, b1], axis=dims[0][1][0]),
        dims,
        preferred_element_type=f32,
    )


def dot_one(a, b):
    return jnp.dot(a.astype(bf16), b.astype(bf16), preferred_element_type=f32)


def split2(x):
    top = x.astype(bf16)
    return top, (x - top.astype(f32)).astype(bf16)


def dot_three(a, b, dims=NN):
    a1, a2 = split2(a)
    b1, b2 = split2(b)
    return lax.dot_general(
        jnp.concatenate([a1, a1, a2], axis=1),
        jnp.concatenate([b1, b2, b1], axis=dims[0][1][0]),
        dims,
        preferred_element_type=f32,
    )


def eye_mask(n=N):
    return lax.broadcasted_iota(jnp.int32, (n, n), 0) == lax.broadcasted_iota(jnp.int32, (n, n), 1)


def total(x):
    return jnp.sum(x)


def unpack(ref):
    blocks = {}
    for k, (i, j) in enumerate(BLOCKS):
        block = ref[k * B : (k + 1) * B, :]
        blocks[i, j] = block
        if i != j:
            blocks[j, i] = block.T
    return jnp.concatenate(
        [jnp.concatenate([blocks[i, j] for j in range(3)], axis=1) for i in range(3)], axis=0
    )


def unpack_vector(ref):
    return jnp.concatenate([ref[6 * B + 8 * k : 6 * B + 8 * k + 8, :] for k in range(3)], axis=1)


def pack(ref, square, vector):
    for k, (i, j) in enumerate(BLOCKS):
        ref[k * B : (k + 1) * B, :] = square[i * B : (i + 1) * B, j * B : (j + 1) * B]
    for k in range(3):
        ref[6 * B + 8 * k : 6 * B + 8 * k + 8, :] = vector[:, k * B : (k + 1) * B]


def newton_inverse(a):
    eye = eye_mask()
    diag_col = jnp.sum(jnp.where(eye, a, 0.0), axis=1, keepdims=True)
    diag_row = jnp.sum(jnp.where(eye, a, 0.0), axis=0, keepdims=True)
    inv_col = 1.0 / diag_col
    inv_row = 1.0 / diag_row
    high = jnp.max(jnp.sum(jnp.abs(a), axis=1, keepdims=True) * inv_col)
    ratio = 10.0
    width = 1.0 - 1.0 / ratio
    centre = (1.0 + 1.0 / ratio) / width
    bound = 1.0 / (2.0 * centre * centre - 1.0)
    alpha = 8.0 * centre * bound / (width * high)
    beta = -8.0 * bound / (width * width * high * high)
    x = beta * (inv_col * a * inv_row) + jnp.where(eye, alpha * inv_row, 0.0)
    one = jnp.where(eye, 1.0, 0.0)
    a_low = a.astype(bf16)
    for _ in range(2):
        half = 0.5 * bound * bound
        gain = 1.0 / (1.0 - half)
        bound = half * gain
        r = one - jnp.dot(a_low, x.astype(bf16), preferred_element_type=f32)
        x = gain * (x + dot_one(x, r))
    r = one - dot_three(a, x)
    x = x + dot_one(x, r)

    def more(carry):
        return jnp.logical_and(carry[1] > 1e-5, carry[0] < 40)

    def step(carry):
        count, _, x = carry
        r = jnp.where(eye_mask(), 1.0, 0.0) - dot_hi(a, x)
        return count + 1, total(r * r), x + dot_three(x, r)

    return lax.while_loop(more, step, (jnp.int32(0), jnp.float32(1.0), x))[2]


def log_start(a):
    n = a.shape[0]
    eye = eye_mask(n)
    diag_col = jnp.sum(jnp.where(eye, a, 0.0), axis=1, keepdims=True)
    diag_row = jnp.sum(jnp.where(eye, a, 0.0), axis=0, keepdims=True)
    scaled = lax.rsqrt(diag_col) * a * lax.rsqrt(diag_row)
    high = jnp.max(jnp.sum(jnp.abs(scaled), axis=1, keepdims=True))
    base = total(jnp.log(diag_row)) + n * jnp.max(jnp.log(jnp.full((8, B), high)))
    return base, jnp.where(eye, 1.0, 0.0) - scaled * (1.0 / high)


def log_terms(r, r2, r4):
    c1, c2, c3, c4, c5, c6, c8 = LOG_COEFS
    terms = r * (c2 * r + c3 * r2 + c5 * r4) + r2 * (c4 * r2 + c6 * r4) + c8 * (r4 * r4)
    return total(terms + c1 * jnp.where(eye_mask(r.shape[0]), r, 0.0))


def trace(r):
    return total(jnp.where(eye_mask(r.shape[0]), r, 0.0))


def log_det_ratio(tops, bottoms):
    signs = [1.0] * len(tops) + [-1.0] * len(bottoms)
    bases, rs = zip(*[log_start(a) for a in tops + bottoms])

    def more(carry):
        return jnp.logical_and(carry[1] > 1e-4, carry[0] < 40)

    def step(carry):
        count, _, value, rs, squares = carry
        fourths = tuple(dot_hi(r2, r2) for r2 in squares)
        for sign, r, r2, r4 in zip(signs, rs, squares, fourths):
            value = value + sign * log_terms(r, r2, r4)
        most = trace(squares[0])
        for r2 in squares[1:]:
            most = jnp.maximum(most, trace(r2))
        return count + 1, most, value, squares, fourths

    carry = (jnp.int32(0), jnp.float32(1.0), jnp.float32(0.0), tuple(rs), tuple(dot_hi(r, r) for r in rs))
    _, _, value, rs, _ = lax.while_loop(more, step, carry)
    for sign, base, r in zip(signs, bases, rs):
        value = value + sign * (trace(r) - base)
    return -value


def row_of(row):
    return jnp.where(lax.broadcasted_iota(jnp.int32, (8, N), 0) == 0, row, 0.0)


def diagonal(row):
    return jnp.where(eye_mask(), row, 0.0)


def edge_kernel(scales, factors, edges):
    for k in range(2):
        edges[k * N : (k + 1) * N, :] = diagonal(scales[k : k + 1, :]) + dot_hi(factors[k], factors[k], NT)


def keep_for_log(square, inverse, block, corner):
    block[...] = square[0 : 2 * B, 0 : 2 * B]
    corner[...] = inverse[2 * B :, 2 * B :]


def first_kernel(size, pos, damping, source, spatial, edges, message, root, edges_out, fold, local, block, corner):
    before = edges[0:N, :]
    after = edges[N:TALL, :]
    square = diagonal(damping[1:2, :]) + spatial_gain * dot_hi(spatial[1], spatial[1], NT) + after + before
    after = jnp.where(pos[0] < size - 1, after, 0.0)
    edges_out[0:N, :] = before
    edges_out[N:TALL, :] = after
    inverse = newton_inverse(square)
    keep_for_log(square, inverse, block, corner)
    root[...] = inverse
    z = dot_hi(row_of(source[1:2, :]), inverse)
    local[...] = z
    after = edges_out[N:TALL, :]
    right = dot_three(after, inverse)
    fold[...] = right
    pack(message, after - dot_three(right, after, NT), dot_hi(z, after, NT))


def second_kernel(
    pos, damping, source, spatial, root, edges, fold, local,
    stack, link, state, own_stack, own, block, corner,
):
    for empty in (own_stack, own, block, corner):
        empty[...] = jnp.zeros(empty.shape, f32)
    before = edges[0:N, :]
    left = dot_hi(before, root[...])
    stack[0:N, :] = left
    stack[N:TALL, :] = fold[...]
    odd = pos[0] % 2 == 1
    link[...] = dot_hi(jnp.where(odd, fold[...], left), jnp.where(odd, before, edges[N:TALL, :]), NT)
    square = diagonal(damping[0:1, :]) + spatial_gain * dot_hi(spatial[0], spatial[0], NT) + before
    vector = row_of(source[0:1, :]) + dot_hi(local[...], before, NT)
    pack(state, square - dot_hi(stack[0:N, :], before, NT), vector)


def invert_kernel(test, pos, state, prior, prior_block, prior_corner, after, *rest):
    *received, new_state, inverse, local, block, corner = rest
    new_state[...] = sum([r[...] for r in received], state[...])

    @pl.when(test(pos[0]))
    def _():
        square = unpack(new_state)
        inv = newton_inverse(square)
        inverse[...] = inv
        keep_for_log(square, inv, block, corner)
        local[...] = dot_hi(unpack_vector(new_state), inv)

    @pl.when(jnp.logical_not(test(pos[0])))
    def _():
        local[...] = prior[...]
        block[...] = prior_block[...]
        corner[...] = prior_corner[...]


def product_kernel(test, side, pos, local, inverse, near, far, prior, stack, left, right, one, other):
    @pl.when(test(pos[0]))
    def _():
        z = local[...]
        parts = []
        for k, (edge, out) in enumerate(((near, left), (far, right))):
            part = dot_three(edge[...], inverse[...])
            stack[k * N : (k + 1) * N, :] = part
            pack(out, -dot_three(part, edge[...], NT), dot_three(z, edge[...], NT))
        up = side(pos[0])
        one[...] = jnp.where(up, stack[N:TALL, :], stack[0:N, :])
        other[...] = jnp.where(up, near[...], far[...])

    @pl.when(jnp.logical_not(test(pos[0])))
    def _():
        stack[...] = prior[...]


def link_kernel(test, pos, one, other, link):
    @pl.when(test(pos[0]))
    def _():
        link[...] = dot_three(one[...], other[...], NT)


def forward_kernel(message, after, out):
    out[...] = message[...]


def last_kernel(test, pos, local, inverse, near, other, prior, stack, state):
    @pl.when(test(pos[0]))
    def _():
        part = dot_three(near[...], inverse[...])
        stack[0:N, :] = part
        stack[N:TALL, :] = jnp.zeros((N, N), f32)
        pack(state, -dot_three(part, near[...], NT), dot_three(local[...], near[...], NT))
        state[...] = state[...] + other[...]

    @pl.when(jnp.logical_not(test(pos[0])))
    def _():
        stack[...] = prior[...]


def root_kernel(test, pos, state, block, corner, value):
    @pl.when(test(pos[0]))
    def _():
        square = unpack(state)
        inv = newton_inverse(square)
        keep_for_log(square, inv, block, corner)
        value[...] = dot_hi(unpack_vector(state), inv)


def log_kernel(test, pairs, pos, after, *rest):
    *refs, logs = rest
    tops, bottoms, came = refs[:pairs], refs[pairs : 2 * pairs], refs[2 * pairs :]
    logs[...] = sum([c[...] for c in came], jnp.zeros((8, B), f32))
    if pairs:

        @pl.when(test(pos[0]))
        def _():
            logs[...] = logs[...] + log_det_ratio([t[...] for t in tops], [b[...] for b in bottoms])


def descend_kernel(test, pos, local, left, current, stack, *rest):
    *right, value = rest

    @pl.when(test(pos[0]))
    def _():
        both = left[...]
        part = stack[0:N, :]
        if right:
            both = jnp.concatenate([left[...], right[0][...]], axis=1)
            part = stack[...]
        found = local[...] + dot_hi(both, part)
        value[...] = jnp.where(log_rows(), left[...], found)

    @pl.when(jnp.logical_not(test(pos[0])))
    def _():
        value[...] = current[...]


def log_rows():
    return lax.broadcasted_iota(jnp.int32, (8, N), 0) == 1


def join_kernel(value, logs, joined):
    joined[...] = jnp.where(log_rows(), jnp.concatenate([logs[0:1, :]] * 3, axis=1), value[...])


def top_kernel(test, pos, local, first, stack, both):
    @pl.when(test(pos[0]))
    def _():
        found = local[...] + dot_hi(first[...], stack[0:N, :])
        both[0:8, :] = jnp.where(log_rows(), first[...], found)
        both[8:16, :] = first[...]

    @pl.when(jnp.logical_not(test(pos[0])))
    def _():
        both[...] = jnp.zeros((16, N), f32)


def second_value_kernel(half, pos, both, came, value):
    value[...] = jnp.where(pos[0] == half, both[0:8, :], jnp.where(pos[0] == 0, came[...], 0.0))


def descend_both_kernel(test, pos, local, both, left, current, stack, value):
    test_first, test_any = test
    first = test_first(pos[0])
    near = jnp.where(first, both[8:16, :], left[...])
    far = jnp.where(first, both[0:8, :], 0.0)
    found = local[...] + dot_hi(jnp.concatenate([near, far], axis=1), stack[...])
    value[...] = jnp.where(test_any(pos[0]), jnp.where(log_rows(), near, found), current[...])


def output_kernel(scale, local, left, right, stack, solution, logs):
    both = jnp.concatenate([left[...], right[...]], axis=1)
    second = local[...] + dot_hi(both, stack[...])
    solution[0:1, :] = left[0:1, :]
    solution[1:2, :] = second[0:1, :]
    logs[...] = left[...] * scale


SMEM = pl.BlockSpec(memory_space=pltpu.SMEM)
VMEM = pl.BlockSpec(memory_space=pltpu.VMEM)
ANY = pl.BlockSpec(memory_space=pl.ANY)


def shape(*dims):
    return jax.ShapeDtypeStruct(dims, f32)


def call(kernel, name, micros, specs, outs, args, aliases={}):
    return pl.pallas_call(
        kernel,
        name=name,
        out_shape=outs,
        in_specs=specs,
        out_specs=[VMEM] * len(outs),
        input_output_aliases=aliases,
        cost_estimate=pl.CostEstimate(
            flops=int(micros * 1.0e9), bytes_accessed=int(micros * 3.0e6), transcendentals=0
        ),
        compiler_params=pltpu.CompilerParams(vmem_limit_bytes=VMEM_LIMIT),
    )(*args)


PACKED = shape(ROWS, B)
SQUARE = shape(N, N)
TWO = shape(TALL, N)
VECTOR = shape(8, N)
BLOCK = shape(2 * B, 2 * B)
CORNER = shape(B, B)


def local(damping, spatial_factor, edge_scale, edge_factor, forcing):
    size = lax.axis_size("tm")
    half = size // 2
    pos = jnp.reshape(lax.axis_index("tm").astype(jnp.int32), (1,))

    def send(x, pairs):
        return lax.ppermute(x, "tm", [p for p in pairs if 0 <= p[1] < size])

    def odd_of(span):
        return lambda p: p % (2 * span) == span

    def ways(span):
        if span == 0:
            return []
        odd = range(span, size, 2 * span)
        if span in (2, 8):
            return [[(i, i - span // 2) for i in odd], [(i - span // 2, i - span) for i in odd]]
        return [[(i, i - span) for i in odd]]

    def follow(x, hops):
        for hop in hops:
            x = send(x, hop)
        return x

    def log_of(test, pairs, after, *args):
        (logs,) = call(
            functools.partial(log_kernel, test, pairs), "log", 0.2, [SMEM, ANY] + [VMEM] * len(args),
            [shape(8, B)], (pos, after) + args,
        )
        return logs

    (edges,) = call(edge_kernel, "edges", 3, [VMEM] * 2, [TWO], (edge_scale, edge_factor))
    message, root, edges, fold, local1, block1, corner1 = call(
        functools.partial(first_kernel, size), "first", 9, [SMEM] + [VMEM] * 4,
        [PACKED, SQUARE, TWO, SQUARE, VECTOR, BLOCK, CORNER],
        (pos, damping, forcing, spatial_factor, edges),
    )
    received = [send(message, [(i, i + 1) for i in range(size)])]
    stack1, link, state, stack, own, block, corner = call(
        second_kernel, "second", 5, [SMEM] + [VMEM] * 7, [TWO, SQUARE, PACKED, TWO, VECTOR, BLOCK, CORNER],
        (pos, damping, forcing, spatial_factor, root, edges, fold, local1),
    )
    near = send(link, [(i, i + 1) for i in range(0, size, 2)])
    far = link
    after = block1
    span = 1
    while span < size:
        step = 2 * span
        active = odd_of(span)
        state, inverse, own, block, corner = call(
            functools.partial(invert_kernel, active), "invert", 1 if len(ways(span // 2)) == 2 else 6,
            [SMEM] + [VMEM] * 4 + [ANY] + [VMEM] * len(received), [PACKED, SQUARE, VECTOR, BLOCK, CORNER],
            (pos, state, own, block, corner, after, *received), {2: 2, 3: 3, 4: 4},
        )
        odd = range(span, size, step)
        if step < size:
            stack, to_left, to_right, one, other = call(
                functools.partial(product_kernel, active, lambda p, step=step: (p // step) % 2 == 1),
                "product", 6, [SMEM] + [VMEM] * 5, [TWO, PACKED, PACKED, SQUARE, SQUARE],
                (pos, own, inverse, near, far, stack), {5: 0},
            )
            left_ways = ways(span)
            between = send(to_left, left_ways[0])
            received = [between, send(to_right, [(i, i + span) for i in odd])]
            (link,) = call(
                functools.partial(link_kernel, active), "link", 3, [SMEM] + [VMEM] * 2, [SQUARE],
                (pos, one, other),
            )
            if len(left_ways) == 2:
                (between,) = call(forward_kernel, "forward", 0.2, [VMEM, ANY], [PACKED], (between, link))
                received[0] = send(between, left_ways[1])
            near = send(link, [(i, i + span) for i in odd if (i // step) % 2 == 0])
            far = send(link, [(i, i - span) for i in odd if (i // step) % 2 == 1])
        else:
            other = send(state, [(0, half)])
            stack, last = call(
                functools.partial(last_kernel, active), "last", 6, [SMEM] + [VMEM] * 5, [TWO, PACKED],
                (pos, own, inverse, near, other, stack), {5: 0},
            )
        if span == 1:
            after = log_of(lambda p: p >= 0, 1, one, block1, corner1)
            logs = [after]
        else:
            before = span // 2
            after = log_of(odd_of(before), 1, between if step < size else inverse, block, corner, *logs)
            logs = [after, follow(after, ways(before))]
        span = step
    at_half = odd_of(half)
    last_block, last_corner, first_value = call(
        functools.partial(root_kernel, at_half), "root", 6, [SMEM, VMEM], [BLOCK, CORNER, VECTOR], (pos, last),
    )
    total_logs = log_of(None, 0, last, *logs)
    came = send(total_logs, [(0, half)])
    logs = log_of(at_half, 2, last, block, last_block, corner, last_corner, total_logs, came)
    (first_value,) = call(join_kernel, "join", 0.2, [VMEM] * 2, [VECTOR], (first_value, logs))
    (both,) = call(
        functools.partial(top_kernel, at_half), "top", 1, [SMEM] + [VMEM] * 3, [shape(16, N)],
        (pos, own, first_value, stack),
    )
    came = send(first_value, [(half, 0)])
    (value,) = call(
        functools.partial(second_value_kernel, half), "value", 0.2, [SMEM] + [VMEM] * 2, [VECTOR], (pos, both, came)
    )
    span = half
    while span > 1:
        step = span
        span //= 2
        odd = range(span, size, step)
        left_value = send(value, [(i - span, i) for i in odd])
        if step == half:
            both = send(both, [(half, span)])
            tests = (lambda p, span=span: p == span, odd_of(span))
            (value,) = call(
                functools.partial(descend_both_kernel, tests), "descend", 1, [SMEM] + [VMEM] * 5, [VECTOR],
                (pos, own, both, left_value, value, stack),
            )
        else:
            right_value = send(value, [(i + span, i) for i in odd if i + span < size])
            (value,) = call(
                functools.partial(descend_kernel, odd_of(span)), "descend", 1, [SMEM] + [VMEM] * 5, [VECTOR],
                (pos, own, left_value, value, stack, right_value),
            )
    right_value = send(value, [(i + 1, i) for i in range(size - 1)])
    solution, logs = call(
        functools.partial(output_kernel, 1.0 / (size * 2 * N)), "output", 1, [VMEM] * 4, [shape(2, N), VECTOR],
        (local1, value, right_value, stack1),
    )
    return (solution, logs[1, 0:1])


def solution(mesh):
    return jax.shard_map(
        local,
        mesh=mesh,
        in_specs=(
            P(("hyp", "tm"), None),
            P(("hyp", "tm"), None, None),
            P(("hyp", "tm"), None),
            P(("hyp", "tm"), None, None),
            P(("hyp", "tm"), None),
        ),
        out_specs=(P(("hyp", "tm"), None), P("hyp")),
        check_vma=False,
    )
```
